32 devices in a mesh: fsdp: 8 (over z, x), rep: 4 (over y, core).
Axes of the slice: x: 2, y: 2, z: 4, core: 2. Of those that a mesh axis runs over, the one named last changes fastest.
Arguments:
- hidden_in: bfloat16 [16384, 768], P(('fsdp', 'rep')), may hold values from -6 to 6
- cotangent: bfloat16 [16384, 768], P(('fsdp', 'rep')), may hold values from -6 to 6
- lengths: int32 [32], P(('fsdp', 'rep')), may hold values from 1 to 512, as said below
- norm_gain: bfloat16 [768], P('fsdp'), may hold values from 0.5 to 1.5
- in_weight: bfloat16 [768, 3352], P('fsdp'), may hold values from -0.21875 to 0.21875
- conv_weight: bfloat16 [4, 1792], P(None, 'fsdp'), may hold values from -3 to 3
- conv_bias: bfloat16 [1792], P('fsdp'), may hold values from -2 to 2
- step_bias: float32 [24], replicated, may hold values from -6 to -2
- decay_log: float32 [24], replicated, may hold values from 0 to 2.77
- skip_weight: float32 [24], replicated, may hold values from 0.5 to 1.5
- mix_gain: bfloat16 [1536], P('fsdp'), may hold values from 0.5 to 1.5
- out_weight: bfloat16 [1536, 768], P('fsdp'), may hold values from -0.15625 to 0.15625
Outputs:
- block_out: bfloat16 [16384, 768], P(('fsdp', 'rep'))
- grad_in: float32 [16384, 768], P(('fsdp', 'rep'))
- grad_norm_gain: float32 [768], P('fsdp')
- grad_in_weight: float32 [768, 3352], P('fsdp')
- grad_conv_weight: float32 [4, 1792], P(None, 'fsdp')
- grad_conv_bias: float32 [1792], P('fsdp')
- grad_step_bias: float32 [24], replicated
- grad_decay_log: float32 [24], replicated
- grad_skip_weight: float32 [24], replicated
- grad_mix_gain: float32 [1536], P('fsdp')
- grad_out_weight: float32 [1536, 768], P('fsdp')
The draws below stay inside these ranges and needn't reach their ends.
Inputs may be any that keep to these rules, and one draw needn't show every extreme that they name: lengths[s] is the number of live tokens of sequence s, which fill its first slots; some sequence has 512 live tokens.
All inputs are finite; a program needn't handle non-finite values.
Results may differ from the reference program's by a relative error of at most 0.0068.
Values may be sent and summed in bfloat16 or wider, within the bound.
A program may use at most 192 MiB of HBM per device.

```python
import jax
import jax.numpy as jnp
from jax import lax

D = 768
NH = 24
HD = 64
NS = 128
KCONV = 4
SEQ_LEN = 512
DI = 1536
CONV_CH = 1792
PROJ = 3352
SEQS = 32
TOKENS = 16384


def draw_lengths(key, part):
    first_key, second_key, third_key = jax.random.split(jax.random.fold_in(key, 17), 3)
    first = jax.random.randint(first_key, (SEQS,), 1, SEQ_LEN + 1)
    second = jax.random.randint(second_key, (SEQS,), 1, SEQ_LEN + 1)
    picked = jax.random.randint(third_key, (), 0, SEQS)
    counts = jnp.minimum(first, second)
    counts = jnp.where(jnp.arange(SEQS) == picked, SEQ_LEN, counts)
    return counts.astype(jnp.int32)


def block_levels(key, shape, cuts, low, top_value):
    def one(dim, blocks):
        steps = jax.random.uniform(jax.random.fold_in(jax.random.fold_in(key, 6), dim), (blocks,), jnp.float32, low / len(cuts), top_value / len(cuts))
        return jnp.repeat(jnp.exp(steps), shape[dim] // blocks).reshape((-1,) + (1,) * (len(shape) - dim - 1))

    level = one(*cuts[0])
    for cut in cuts[1:]:
        level = level * one(*cut)
    return level


def bell_draw(key, dims, scale, most, cuts=(), kind=jnp.bfloat16):
    array = jax.random.normal(key, dims, jnp.float32) * scale
    if len(cuts) > 0:
        array = block_levels(key, dims, cuts, -0.22, 0.18) * array
    return jnp.clip(array, min=-most, max=most).astype(kind)


def setup_inputs(seed: int = 0) -> dict:
    streams_of = jax.random.split(jax.random.key(seed), 13)
    return {
        "hidden_in": bell_draw(streams_of[0], (TOKENS, D), 1.0, 6.0, ((0, 32),)),
        "cotangent": bell_draw(streams_of[1], (TOKENS, D), 1.0, 6.0, ((0, 32),)),
        "lengths": draw_lengths(jax.random.fold_in(streams_of[12], 71), 0),
        "norm_gain": jnp.clip(1.0 + 0.1 * jax.random.normal(streams_of[3], (D,), jnp.float32), 0.5, 1.5).astype(jnp.bfloat16),
        "in_weight": bell_draw(streams_of[4], (D, PROJ), D ** -0.5, 0.21875, ((0, 8),)),
        "conv_weight": bell_draw(streams_of[5], (KCONV, CONV_CH), 0.5, 3.0, ((1, 8),)),
        "conv_bias": bell_draw(streams_of[6], (CONV_CH,), 0.3, 2.0, ((0, 8),)),
        "step_bias": jnp.clip(jax.random.uniform(streams_of[7], (NH,), jnp.float32, -6.0, -2.0), -6.0, -2.0),
        "decay_log": jnp.clip(jax.random.uniform(streams_of[8], (NH,), jnp.float32, 0.0, 2.77), 0.0, 2.77),
        "skip_weight": jnp.clip(jax.random.uniform(streams_of[9], (NH,), jnp.float32, 0.5, 1.5), 0.5, 1.5),
        "mix_gain": jnp.clip(1.0 + 0.1 * jax.random.normal(streams_of[10], (DI,), jnp.float32), 0.5, 1.5).astype(jnp.bfloat16),
        "out_weight": bell_draw(streams_of[11], (DI, D), DI ** -0.5, 0.15625, ((0, 8),)),
    }


EPS = 1e-05
HIGH = lax.Precision.HIGHEST

def pre_norm(rows, gain):
    scale = lax.rsqrt(lax.optimization_barrier(jnp.mean(rows * rows, axis=-1, keepdims=True)) + EPS)
    return rows * scale * gain

def quadratic_scan(values, step, logdecay, keys_b, query_c):
    length = values.shape[1]
    cumlog = jnp.cumsum(logdecay, axis=1)
    spread = cumlog[:, :, None, :] - cumlog[:, None, :, :]
    causal = (jnp.arange(length)[:, None] >= jnp.arange(length)[None, :])[None, :, :, None]
    decay = jnp.exp(jnp.where(causal, spread, -jnp.inf))
    intersection = jnp.einsum('stn,sun->stu', query_c, keys_b, precision=HIGH)
    scaled = values * step[..., None]
    return jnp.einsum('stuh,suhp->sthp', intersection[..., None] * decay, scaled, precision=HIGH)

def mixer_core(proj, conv_w, conv_b, step_bias, decay_log, skip_weight, mix_gain, scan_fn):
    seqs_here = proj.shape[0]
    length = proj.shape[1]
    gate = proj[..., :DI]
    conv_in = proj[..., DI:DI + CONV_CH]
    step_raw = proj[..., DI + CONV_CH:]
    padded = jnp.pad(conv_in, ((0, 0), (KCONV - 1, 0), (0, 0)))
    conv_out = jnp.zeros_like(conv_in) + conv_b
    for offset in range(KCONV):
        conv_out = conv_out + conv_w[offset] * padded[:, offset:offset + length]
    active = jax.nn.silu(conv_out)
    values = active[..., :DI].reshape(seqs_here, length, NH, HD)
    keys_b = active[..., DI:DI + NS]
    query_c = active[..., DI + NS:]
    step = jax.nn.softplus(step_raw + step_bias)
    logdecay = -step * jnp.exp(decay_log)
    mixed = scan_fn(values, step, logdecay, keys_b, query_c)
    mixed = mixed + skip_weight[:, None] * values
    flat = mixed.reshape(seqs_here, length, DI) * jax.nn.silu(gate)
    scale = lax.rsqrt(lax.optimization_barrier(jnp.mean(flat * flat, axis=-1, keepdims=True)) + EPS)
    return flat * scale * mix_gain

def reference(hidden_in, cotangent, lengths, norm_gain, in_weight, conv_weight, conv_bias, step_bias, decay_log, skip_weight, mix_gain, out_weight):
    gain_one = norm_gain.astype(jnp.float32)
    conv_w = conv_weight.astype(jnp.float32)
    conv_b = conv_bias.astype(jnp.float32)
    mix_full = mix_gain.astype(jnp.float32)
    rows_all = hidden_in.reshape(SEQS, SEQ_LEN, D)
    cots_all = cotangent.reshape(SEQS, SEQ_LEN, D)

    def core(proj, cw, cb, sb, dl, sk, mg):
        return mixer_core(proj[None], cw, cb, sb, dl, sk, mg, quadratic_scan)[0]

    def one_seq(carry, item):
        rows, cots, count = item
        resid = rows.astype(jnp.float32)
        normed, norm_back = jax.vjp(pre_norm, resid, gain_one)
        normed_b = normed.astype(jnp.bfloat16)
        proj = jnp.dot(normed_b, in_weight, preferred_element_type=jnp.float32)
        gated, core_back = jax.vjp(core, proj, conv_w, conv_b, step_bias, decay_log, skip_weight, mix_full)
        gated_b = gated.astype(jnp.bfloat16)
        branch = jnp.dot(gated_b, out_weight, preferred_element_type=jnp.float32)
        live = (jnp.arange(SEQ_LEN) < count).astype(jnp.float32)[:, None]
        out_rows = (resid + live * branch).astype(jnp.bfloat16)
        cot_live = cots * live.astype(jnp.bfloat16)
        d_gated = jnp.dot(cot_live, out_weight.T, preferred_element_type=jnp.float32)
        d_out_w = jnp.dot(gated_b.T, cot_live, preferred_element_type=jnp.float32)
        d_proj, d_cw, d_cb, d_sb, d_dl, d_sk, d_mg = core_back(d_gated)
        d_proj_b = d_proj.astype(jnp.bfloat16)
        d_in_w = jnp.dot(normed_b.T, d_proj_b, preferred_element_type=jnp.float32)
        d_normed = jnp.dot(d_proj_b, in_weight.T, preferred_element_type=jnp.float32)
        d_resid, d_gain = norm_back(d_normed)
        grad_rows = cots.astype(jnp.float32) + d_resid
        terms = (d_gain, d_in_w, d_cw, d_cb, d_sb, d_dl, d_sk, d_mg, d_out_w)
        return (tuple((left + right for left, right in zip(carry, terms))), (out_rows, grad_rows))
    start = (jnp.zeros((D,), jnp.float32), jnp.zeros((D, PROJ), jnp.float32), jnp.zeros((KCONV, CONV_CH), jnp.float32), jnp.zeros((CONV_CH,), jnp.float32), jnp.zeros((NH,), jnp.float32), jnp.zeros((NH,), jnp.float32), jnp.zeros((NH,), jnp.float32), jnp.zeros((DI,), jnp.float32), jnp.zeros((DI, D), jnp.float32))
    grads, (out_all, grad_all) = lax.scan(one_seq, start, (rows_all, cots_all, lengths))
    g_gain, g_in, g_cw, g_cb, g_sb, g_dl, g_sk, g_mg, g_out = grads
    return (out_all.reshape(TOKENS, D), grad_all.reshape(TOKENS, D), g_gain, g_in, g_cw, g_cb, g_sb, g_dl, g_sk, g_mg, g_out)
```

```python
import functools


import jax
import jax.numpy as jnp
from jax import lax
from jax.experimental import pallas as pl
from jax.experimental.pallas import tpu as pltpu
from jax.sharding import PartitionSpec as P

NH = 24
HD = 64
NS = 128
KCONV = 4
DI = 1536
CONV_CH = 1792
PROJ = 3352
LANES = 128
PAIR = LANES // HD

EPS = 1e-05
HIGH = lax.Precision.HIGHEST


def contract(left, right, left_dim, right_dim, precision=None):
    return lax.dot_general(
        left,
        right,
        (((left_dim,), (right_dim,)), ((), ())),
        precision=precision,
        preferred_element_type=jnp.float32,
    )


LOG2E = 1.4426950408889634
QLEN = 128
GROUP = 3


def split_hi_lo(value):
    high = value.astype(jnp.bfloat16)
    return high, (value - high.astype(jnp.float32)).astype(jnp.bfloat16)


def row_loop(total, size, step):
    def one(i, carry):
        step(pl.multiple_of(i * size, size))
        return carry

    lax.fori_loop(0, total // size, one, 0)


def fold(value):
    return jnp.sum(value.reshape(-1, 8, value.shape[-1]), axis=0)


def head_expander(width):
    row = lax.broadcasted_iota(jnp.int32, (LANES, width), 0)
    col = lax.broadcasted_iota(jnp.int32, (LANES, width), 1)
    return jnp.where(row % HD == col // HD, 1.0, 0.0).astype(jnp.bfloat16)


def head_summer(width):
    row = lax.broadcasted_iota(jnp.int32, (width, LANES), 0)
    col = lax.broadcasted_iota(jnp.int32, (width, LANES), 1)
    return jnp.where(row // HD == col, 1.0, 0.0).astype(jnp.bfloat16)


def two_part(value):
    high = value.astype(jnp.bfloat16).astype(jnp.float32)
    low = pltpu.roll(value - high, HD, 1)
    lane = lax.broadcasted_iota(jnp.int32, value.shape, 1)
    return jnp.where(lane < HD, high, low).astype(jnp.bfloat16)


def stage_norm(r):
    total = r.hidden.shape[0]

    def step(at):
        rows = pl.ds(at, 64)
        h = r.hidden[rows, :].astype(jnp.float32)
        scale = lax.rsqrt(jnp.mean(h * h, axis=-1, keepdims=True) + EPS)
        r.nb[rows, :] = (h * scale * r.gain[...]).astype(jnp.bfloat16)

    row_loop(total, 64, step)
    r.nbt[...] = r.nb[...].T
    r.expand[...] = head_expander(DI)
    r.summer[...] = head_summer(DI)


def stage_proj_x(r, k):
    total = r.hidden.shape[0]
    width = r.wx[k].shape[1]
    r.raw[8 : 8 + total, k * width : (k + 1) * width] = contract(r.nb[...], r.wx[k][...], 1, 0)


def stage_conv(r):
    total = r.hidden.shape[0]
    r.raw[0:8, :] = jnp.zeros((8, r.raw.shape[1]), jnp.float32)
    size, wide = 64, 256

    def step(at):
        for lanes in range(0, CONV_CH, wide):
            cols = slice(lanes, lanes + wide)
            block = r.raw[pl.ds(at, size + 8), cols]
            conv = jnp.zeros((size, wide), jnp.float32) + r.cb[:, cols]
            for k in range(KCONV):
                start = 8 - (KCONV - 1) + k
                conv = conv + r.cw[k : k + 1, cols] * block[start : start + size]
            sig = jax.nn.sigmoid(conv)
            act = conv * sig
            r.act[pl.ds(at, size), cols] = act
            r.dsil[pl.ds(at, size), cols] = sig + act * (1.0 - sig)

    row_loop(total, size, step)


def stage_steps(r):
    total = r.hidden.shape[0]
    lane = lax.broadcasted_iota(jnp.int32, (1, LANES), 1)
    rate = jnp.where(lane < NH, jnp.exp(r.dl[...]), 0.0)
    row = lax.broadcasted_iota(jnp.int32, (QLEN, QLEN), 0)
    col = lax.broadcasted_iota(jnp.int32, (QLEN, QLEN), 1)
    lower = jnp.where(row >= col, 1.0, 0.0)

    def step(at):
        rows = pl.ds(at, QLEN)
        pre = r.raw[pl.ds(at + 8, QLEN), CONV_CH : CONV_CH + LANES] + r.sb[...]
        dt = jnp.maximum(pre, 0.0) + jnp.log1p(jnp.exp(-jnp.abs(pre)))
        dt = jnp.where(lane < NH, dt, 0.0)
        r.dt[rows, :] = dt
        r.sgd[rows, :] = jax.nn.sigmoid(pre)
        cum = contract(lower, -dt * rate, 1, 0, lax.Precision.HIGHEST) * LOG2E
        r.cum[rows, :] = cum
        r.cumt[rows, :] = cum.T

    row_loop(total, QLEN, step)


def chunk_factors(r, rows):
    cum = r.cum[rows, :]
    last = cum[QLEN - 1 : QLEN, :]
    stack = jnp.concatenate(
        [two_part(r.dt[rows, :]), two_part(jnp.exp2(cum)), two_part(jnp.exp2(last - cum))], axis=0
    )
    half = DI // 2
    for side in range(2):
        cols = slice(side * half, (side + 1) * half)
        r.ex[0 : 3 * QLEN, cols] = contract(stack, r.expand[:, cols], 1, 0)


def halves(value):
    lane = lax.broadcasted_iota(jnp.int32, value.shape, 1)
    zero = jnp.zeros_like(value)
    return jnp.concatenate(
        [jnp.where(lane < HD, value, zero), jnp.where(lane >= HD, value, zero)], axis=0
    )


def stage_scan(r):
    total = r.hidden.shape[0]
    row = lax.broadcasted_iota(jnp.int32, (QLEN, QLEN), 0)
    col = lax.broadcasted_iota(jnp.int32, (QLEN, QLEN), 1)
    r.state[...] = jnp.zeros_like(r.state)

    def step(at):
        rows = pl.ds(at, QLEN)
        keys = r.act[rows, DI : DI + NS]
        query = r.act[rows, DI + NS : DI + 2 * NS]
        score = jnp.where(row >= col, contract(query, keys, 1, 1, lax.Precision.HIGHEST), 0.0)
        query_b = query.astype(jnp.bfloat16)
        keys_t = keys.T.astype(jnp.bfloat16)
        chunk_factors(r, rows)
        r.states[rows, :] = r.state[...].astype(jnp.bfloat16)
        cum = r.cum[rows, :]
        cumt = r.cumt[rows, :]
        for p in range(NH // PAIR):
            cols = slice(p * LANES, (p + 1) * LANES)
            x = r.act[rows, cols]
            scaled_f = x * r.ex[0:QLEN, cols]
            scaled = scaled_f.astype(jnp.bfloat16)
            tail = (scaled_f * r.ex[2 * QLEN : 3 * QLEN, cols]).astype(jnp.bfloat16)
            parts = []
            for sub in range(PAIR):
                head = p * PAIR + sub
                spread = cum[:, head : head + 1] - cumt[head : head + 1, :]
                parts.append((score * jnp.exp2(jnp.minimum(spread, 0.0))).astype(jnp.bfloat16))
            inner = contract(jnp.concatenate(parts, axis=1), halves(scaled), 1, 0)
            lead = r.ex[QLEN : 2 * QLEN, cols]
            outer = contract(query_b, r.states[rows, cols], 1, 0)
            r.ysc[rows, cols] = inner + lead * outer
            r.state[:, cols] = lead[QLEN - 1 : QLEN, :] * r.state[:, cols] + contract(
                keys_t, tail, 1, 0
            )

    row_loop(total, QLEN, step)


def stage_proj_z(r, k):
    width = r.wz[k].shape[1]
    r.z[:, k * width : (k + 1) * width] = contract(r.nb[...], r.wz[k][...], 1, 0)


def stage_gate(r):
    total = r.hidden.shape[0]
    size = 16
    r.skx[...] = contract(two_part(jnp.broadcast_to(r.sk[...], (8, LANES))), r.expand[...], 1, 0)

    def step(at):
        rows = pl.ds(at, size)
        y = r.ysc[rows, :] + r.skx[0:1, :] * r.act[rows, 0:DI]
        z = r.z[rows, :]
        q = y * (z * jax.nn.sigmoid(z))
        scale = lax.rsqrt(jnp.mean(q * q, axis=-1, keepdims=True) + EPS)
        r.gb[rows, :] = (q * scale * r.mg[...]).astype(jnp.bfloat16)
        r.r2[rows, :] = jnp.broadcast_to(scale, (size, LANES))

    row_loop(total, size, step)


def live_rows(r, at, size):
    position = lax.broadcasted_iota(jnp.int32, (size, 1), 0) + at
    return jnp.where(position < r.count[0], 1.0, 0.0)


def stage_out(r):
    total, wide = r.hidden.shape

    def step(at):
        rows = pl.ds(at, 64)
        live = live_rows(r, at, 64)
        r.cl[rows, :] = (r.cot[rows, :].astype(jnp.float32) * live).astype(jnp.bfloat16)

    row_loop(total, 64, step)
    parts = len(r.wo)
    width = wide // parts
    for k in range(parts):
        cols = slice(k * width, (k + 1) * width)
        branch = contract(r.gb[...], r.wo[k][...], 1, 0)
        live = live_rows(r, 0, total)
        r.block_out[:, cols] = (r.hidden[:, cols].astype(jnp.float32) + live * branch).astype(
            jnp.bfloat16
        )
    block = 256
    for at in range(0, DI, block):
        sums = None
        for k in range(parts):
            cols = slice(k * width, (k + 1) * width)
            term = contract(r.cl[:, cols], r.wo[k][at : at + block, :], 1, 1)
            sums = term if sums is None else sums + term
        r.dy[:, at : at + block] = sums


def stage_grad_out(r, k):
    width = r.gwo[k].shape[1]
    part = contract(r.gb[...], r.cl[:, k * width : (k + 1) * width], 0, 0)
    r.gwo[k][...] = part.astype(jnp.bfloat16)


def stage_gate_back(r):
    total = r.hidden.shape[0]
    size = 16
    r.acc_mg[...] = jnp.zeros_like(r.acc_mg)
    r.acc_sk[...] = jnp.zeros_like(r.acc_sk)

    def step(at):
        rows = pl.ds(at, size)
        x = r.act[rows, 0:DI]
        y = r.ysc[rows, :] + r.skx[0:1, :] * x
        z = r.z[rows, :]
        sig = jax.nn.sigmoid(z)
        gate = z * sig
        q = y * gate
        scale = r.r2[rows, 0:1]
        dg = r.dy[rows, :]
        r.acc_mg[...] += fold(dg * q * scale)
        dn = dg * r.mg[...]
        mean = jnp.sum(dn * q, axis=-1, keepdims=True) * (1.0 / DI)
        dq = scale * (dn - q * (scale * scale * mean))
        dy = dq * gate
        r.dy[rows, :] = dy
        r.acc_sk[...] += fold(dy * x)
        r.dz[rows, :] = (dq * y * (sig + gate * (1.0 - sig))).astype(jnp.bfloat16)

    row_loop(total, size, step)


def stage_grad_z(r, k):
    width = r.gwz[k].shape[1]
    part = contract(r.nbt[...], r.dz[:, k * width : (k + 1) * width], 1, 0)
    r.gwz[k][...] = part.astype(jnp.bfloat16)


def head_sums(r, values):
    parts = []
    for value in values:
        parts += list(split_hi_lo(value))
    sums = contract(jnp.concatenate(parts, axis=0), r.summer[...], 1, 0)
    out, at = [], 0
    for value in values:
        count = value.shape[0]
        out.append(sums[at : at + count] + sums[at + count : at + 2 * count])
        at += 2 * count
    return out


def stage_scan_back(r):
    total = r.hidden.shape[0]
    chunks = total // QLEN
    row = lax.broadcasted_iota(jnp.int32, (QLEN, QLEN), 0)
    col = lax.broadcasted_iota(jnp.int32, (QLEN, QLEN), 1)
    upper = jnp.where(col >= row, 1.0, 0.0)
    lane = lax.broadcasted_iota(jnp.int32, (1, LANES), 1)
    rate = jnp.where(lane < NH, jnp.exp(r.dl[...]), 0.0)
    r.dstate[...] = jnp.zeros_like(r.dstate)
    r.acc_dl[...] = jnp.zeros_like(r.acc_dl)
    r.acc_sb[...] = jnp.zeros_like(r.acc_sb)

    def step(i, carry):
        at = pl.multiple_of((chunks - 1 - i) * QLEN, QLEN)
        rows = pl.ds(at, QLEN)
        keys = r.act[rows, DI : DI + NS]
        query = r.act[rows, DI + NS : DI + 2 * NS]
        score = jnp.where(col >= row, contract(keys, query, 1, 1, lax.Precision.HIGHEST), 0.0)
        keys_b = keys.astype(jnp.bfloat16)
        query_t = query.T.astype(jnp.bfloat16)
        chunk_factors(r, rows)
        cum = r.cum[rows, :]
        cumt = r.cumt[rows, :]
        r.dscore[...] = jnp.zeros_like(r.dscore)
        r.dkq[...] = jnp.zeros_like(r.dkq)
        for p in range(NH // PAIR):
            cols = slice(p * LANES, (p + 1) * LANES)
            dy = r.dy[rows, cols]
            dy_b = dy.astype(jnp.bfloat16)
            x = r.act[rows, cols]
            scaled_f = x * r.ex[0:QLEN, cols]
            scaled = scaled_f.astype(jnp.bfloat16)
            tail = (scaled_f * r.ex[2 * QLEN : 3 * QLEN, cols]).astype(jnp.bfloat16)
            lead = r.ex[QLEN : 2 * QLEN, cols]
            stacked = halves(dy_b)
            d_mixed = contract(scaled, stacked, 1, 1)
            parts = []
            gain = None
            for sub in range(PAIR):
                head = p * PAIR + sub
                spread = cumt[head : head + 1, :] - cum[:, head : head + 1]
                decay = jnp.exp2(jnp.minimum(spread, 0.0))
                term = d_mixed[:, sub * QLEN : (sub + 1) * QLEN] * decay
                gain = term if gain is None else gain + term
                parts.append((score * decay).astype(jnp.bfloat16))
            r.dscore[...] += gain
            d_state = r.dstate[:, cols]
            d_state_b = d_state.astype(jnp.bfloat16)
            d_scaled = contract(jnp.concatenate(parts, axis=1), stacked, 1, 0)
            d_outer = r.ex[2 * QLEN : 3 * QLEN, cols] * contract(keys_b, d_state_b, 1, 0)
            d_scaled = d_scaled + d_outer
            dy_lead = (dy * lead).astype(jnp.bfloat16)
            r.dkq[:, 0:NS] += contract(tail, d_state_b, 1, 1)
            r.dkq[:, NS : 2 * NS] += contract(dy_lead, r.states[rows, cols], 1, 1)
            kept = lead[QLEN - 1 : QLEN, :] * r.states[rows, cols].astype(jnp.float32)
            across = kept * d_state + scaled.astype(jnp.float32) * d_outer
            r.zrow[0:1, cols] = jnp.sum(across, axis=0, keepdims=True)
            r.dstate[:, cols] = lead[QLEN - 1 : QLEN, :] * d_state + contract(
                query_t, dy_lead, 1, 0
            )
            r.prod[0:QLEN, cols] = (
                dy_b.astype(jnp.float32) * r.ysc[rows, cols]
                - scaled.astype(jnp.float32) * d_scaled
            )
            r.prod[QLEN : 2 * QLEN, cols] = x * d_scaled
            dx = d_scaled * r.ex[0:QLEN, cols] + r.skx[0:1, cols] * dy
            r.act[rows, cols] = dx * r.dsil[rows, cols]
        dscore = jnp.where(col >= row, r.dscore[...], 0.0)
        d_keys = contract(dscore, query, 1, 0, lax.Precision.HIGHEST) + r.dkq[:, 0:NS]
        d_query = contract(dscore.T, keys, 1, 0, lax.Precision.HIGHEST) + r.dkq[:, NS : 2 * NS]
        both = jnp.concatenate([d_keys, d_query], axis=1)
        r.act[rows, DI:CONV_CH] = both * r.dsil[rows, DI:CONV_CH]
        flow, d_dt, across = head_sums(
            r, [r.prod[0:QLEN, :], r.prod[QLEN : 2 * QLEN, :], jnp.broadcast_to(r.zrow[0:1, :], (16, DI))]
        )
        da = contract(upper, flow, 1, 0, lax.Precision.HIGHEST) + across[0:1, :]
        dt = r.dt[rows, :]
        r.acc_dl[...] += fold(-da * dt * rate)
        d_pre = (d_dt - da * rate) * r.sgd[rows, :]
        d_pre = jnp.where(lane < NH, d_pre, 0.0)
        r.acc_sb[...] += fold(d_pre)
        r.dxb[rows, CONV_CH : CONV_CH + LANES] = d_pre.astype(jnp.bfloat16)
        return carry

    lax.fori_loop(0, chunks, step, 0)


def stage_conv_back(r):
    total = r.hidden.shape[0]
    size, wide = 64, 256
    r.act[total : total + 8, :] = jnp.zeros((8, CONV_CH), jnp.float32)
    r.acc_cw[...] = jnp.zeros_like(r.acc_cw)

    def step(at):
        for lanes in range(0, CONV_CH, wide):
            cols = slice(lanes, lanes + wide)
            grads = r.act[pl.ds(at, size + 8), cols]
            inputs = r.raw[pl.ds(at, size + 8), cols]
            here = grads[0:size]
            total_in = None
            for k in range(KCONV):
                shift = KCONV - 1 - k
                term = r.cw[k : k + 1, cols] * grads[shift : shift + size]
                total_in = term if total_in is None else total_in + term
                start = 8 - (KCONV - 1) + k
                r.acc_cw[k * 8 : (k + 1) * 8, cols] += fold(here * inputs[start : start + size])
            r.acc_cw[KCONV * 8 : (KCONV + 1) * 8, cols] += fold(here)
            r.dxb[pl.ds(at, size), cols] = total_in.astype(jnp.bfloat16)

    row_loop(total, size, step)


def stage_grad_x(r, k):
    width = r.gwx[k].shape[1]
    part = contract(r.nbt[...], r.dxb[:, k * width : (k + 1) * width], 1, 0)
    r.gwx[k][...] = part.astype(jnp.bfloat16)


def stage_grad_in(r):
    total, wide = r.hidden.shape
    block = 256
    for at in range(0, wide, block):
        sums = None
        for grads, weights in ((r.dz, r.wz), (r.dxb, r.wx)):
            width = weights[0].shape[1]
            for k in range(len(weights)):
                term = contract(
                    grads[:, k * width : (k + 1) * width], weights[k][at : at + block, :], 1, 1
                )
                sums = term if sums is None else sums + term
        r.grad_in[:, at : at + block] = sums


def stage_norm_back(r):
    total, wide = r.hidden.shape
    r.acc_gain[...] = jnp.zeros_like(r.acc_gain)

    def step(at):
        rows = pl.ds(at, 32)
        h = r.hidden[rows, :].astype(jnp.float32)
        scale = lax.rsqrt(jnp.mean(h * h, axis=-1, keepdims=True) + EPS)
        dn = r.grad_in[rows, :]
        r.acc_gain[...] += fold(dn * (h * scale))
        dn = dn * r.gain[...]
        mean = jnp.sum(dn * h, axis=-1, keepdims=True) * (1.0 / wide)
        r.grad_in[rows, :] = r.cot[rows, :].astype(jnp.float32) + scale * (
            dn - h * (scale * scale * mean)
        )

    row_loop(total, 32, step)


def stage_vectors(r):
    r.vec[...] = jnp.zeros_like(r.vec)
    for k in range(KCONV + 1):
        r.vec[k : k + 1, :] = jnp.sum(r.acc_cw[k * 8 : (k + 1) * 8, :], axis=0, keepdims=True)
    r.vec[5:6, 0:DI] = jnp.sum(r.acc_mg[...], axis=0, keepdims=True)
    wide = r.acc_gain.shape[1]
    r.vec[6:7, 0:wide] = jnp.sum(r.acc_gain[...], axis=0, keepdims=True)
    r.vec[7:8, 0:LANES] = jnp.sum(r.acc_sb[...], axis=0, keepdims=True)
    r.vec[7:8, LANES : 2 * LANES] = jnp.sum(r.acc_dl[...], axis=0, keepdims=True)
    sums = jnp.sum(r.acc_sk[...], axis=0, keepdims=True)
    (heads,) = head_sums(r, [jnp.broadcast_to(sums, (16, DI))])
    r.vec[7:8, 2 * LANES : 3 * LANES] = heads[0:1, :]


class Refs:
    pass


def core_scratch(total, wide):
    f32, bf16 = jnp.float32, jnp.bfloat16
    span = CONV_CH + LANES
    return dict(
        nb=((total, wide), bf16),
        nbt=((wide, total), bf16),
        expand=((LANES, DI), bf16),
        summer=((DI, LANES), bf16),
        raw=((total + 8, span), f32),
        act=((total + 8, CONV_CH), f32),
        dsil=((total, CONV_CH), f32),
        dt=((total, LANES), f32),
        sgd=((total, LANES), f32),
        cum=((total, LANES), f32),
        cumt=((total, LANES), f32),
        state=((NS, DI), f32),
        dstate=((NS, DI), f32),
        states=((total, DI), bf16),
        ysc=((total, DI), f32),
        z=((total, DI), f32),
        skx=((8, DI), f32),
        gb=((total, DI), bf16),
        r2=((total, LANES), f32),
        cl=((total, wide), bf16),
        dy=((total, DI), f32),
        dz=((total, DI), bf16),
        dxb=((total, span), bf16),
        dscore=((QLEN, QLEN), f32),
        dkq=((QLEN, 2 * NS), f32),
        zrow=((8, DI), f32),
        prod=((2 * QLEN, DI), f32),
        acc_mg=((8, DI), f32),
        acc_sk=((8, DI), f32),
        acc_dl=((8, LANES), f32),
        acc_sb=((8, LANES), f32),
        acc_cw=((8 * (KCONV + 1), CONV_CH), f32),
        acc_gain=((8, wide), f32),
    )


def bits_of(axis):
    size = lax.axis_size(axis)
    return [(axis, 1 << k) for k in reversed(range(size.bit_length() - 1))]


def all_labels():
    return bits_of("fsdp") + bits_of("rep")


def my_bit(label):
    return (lax.axis_index(label[0]) // label[1]) % 2


def partner(label):
    ids = {name: lax.axis_index(name) for name in ("fsdp", "rep")}
    ids[label[0]] = ids[label[0]] + label[1] * (1 - 2 * my_bit(label))
    return (ids["fsdp"], ids["rep"])


def greet(labels):
    barrier = pltpu.get_barrier_semaphore()
    for label in labels:
        pl.semaphore_signal(
            barrier, inc=1, device_id=partner(label), device_id_type=pl.DeviceIdType.MESH
        )
    pl.semaphore_wait(barrier, len(labels))


def send(source, target, sems, stream, slot, label):
    copy = pltpu.make_async_remote_copy(
        src_ref=source,
        dst_ref=target,
        send_sem=sems[0].at[stream, slot],
        recv_sem=sems[1].at[stream, slot],
        device_id=partner(label),
        device_id_type=pl.DeviceIdType.MESH,
    )
    copy.start()
    return copy


def orders():
    fsdp, rep = bits_of("fsdp"), bits_of("rep")
    near, wide = fsdp[-1:], fsdp[:-1]
    mid, far = wide[-1:], wide[:-1]
    core, row = rep[-1:], rep[:-1]
    return (
        core + row + near + mid + far,
        core + near + mid + row + far,
        core + mid + row + near + far,
    )


def position(order):
    place = 0
    for label in order:
        place = place * 2 + my_bit(label)
    return place


def gather_kernel(plan, *refs):
    count = len(plan)
    ins, outs = refs[:count], refs[count : 2 * count]
    sems, local = refs[2 * count : 2 * count + 2], refs[2 * count + 2]
    greet(all_labels())
    steps = max(len(order) for order in plan)
    open_sends, waiting, locals_ = [], {}, []
    for k in range(count):
        copy = pltpu.make_async_copy(ins[k], outs[k].at[pl.ds(position(plan[k]), 1)], local.at[k])
        copy.start()
        locals_.append(copy)
    for step in range(steps):
        for k, order in enumerate(plan):
            if step >= len(order):
                continue
            size = 1 << step
            start = position(order) // size * size
            if step == 0:
                source = ins[k]
            else:
                if step == 1:
                    locals_[k].wait()
                waiting[k].wait_recv()
                source = outs[k].at[pl.ds(start, size)]
            label = order[len(order) - 1 - step]
            copy = send(source, outs[k].at[pl.ds(start, size)], sems, k, step, label)
            waiting[k] = copy
            open_sends.append(copy)
    for k in range(count):
        waiting[k].wait_recv()
        if len(plan[k]) < 2:
            locals_[k].wait()
    for copy in open_sends:
        copy.wait_send()


def gather_all(plan, pieces):
    steps = max(len(order) for order in plan)
    vmem = pl.BlockSpec(memory_space=pltpu.VMEM)
    return pl.pallas_call(
        functools.partial(gather_kernel, plan),
        in_specs=[vmem] * len(pieces),
        out_specs=[vmem] * len(pieces),
        out_shape=[
            jax.ShapeDtypeStruct((1 << len(order),) + piece.shape[1:], piece.dtype)
            for order, piece in zip(plan, pieces)
        ],
        scratch_shapes=[
            pltpu.SemaphoreType.DMA((len(pieces), steps)),
            pltpu.SemaphoreType.DMA((len(pieces), steps)),
            pltpu.SemaphoreType.DMA((len(pieces),)),
        ],
        compiler_params=pltpu.CompilerParams(
            collective_id=0, has_side_effects=True, vmem_limit_bytes=60 << 20
        ),
        name="gather_weights",
    )(*pieces)


def reduce_kernel(plan, tail, *refs):
    count = len(plan)
    steps = len(plan[0])
    grads, vector = refs[:count], refs[count]
    outs, total = refs[count + 1 : 2 * count + 1], refs[2 * count + 1]
    at = 2 * count + 2
    held = [refs[at + k * steps : at + (k + 1) * steps] for k in range(count)]
    at += count * steps
    sums = refs[at : at + steps]
    sems, local = refs[at + steps : at + steps + 2], refs[at + steps + 2]
    labels = all_labels()
    greet(labels)
    open_sends, waiting = [], {}
    vector_order = labels[::-1]

    def source_of(k, step):
        return grads[k] if step == 0 else held[k][step - 1]

    def add_in(k, step):
        size = 1 << (steps - 1 - step)
        base = source_of(k, step)
        target = held[k][step]
        start = my_bit(plan[k][step]) * size

        def one(i, carry):
            left = base[start + i].astype(jnp.float32)
            target[i] = (left + target[i].astype(jnp.float32)).astype(target.dtype)
            return carry

        lax.fori_loop(0, size, one, 0)

    for step in range(steps):
        for k in range(count):
            if step > 0:
                waiting[k].wait_recv()
                add_in(k, step - 1)
            label = plan[k][step]
            size = 1 << (steps - 1 - step)
            away = source_of(k, step).at[pl.ds((1 - my_bit(label)) * size, size)]
            waiting[k] = send(away, held[k][step], sems, k, step, label)
            open_sends.append(waiting[k])
        if step > 0:
            waiting[count].wait_recv()
            before = vector if step == 1 else sums[step - 2]
            sums[step - 1][...] = before[...] + sums[step - 1][...]
        now = vector if step == 0 else sums[step - 1]
        waiting[count] = send(now, sums[step], sems, count, step, vector_order[step])
        open_sends.append(waiting[count])

    here = lax.axis_index("rep")
    known = {k: [0] for k in range(count)}
    inbox = {k: [] for k in range(count)}
    for hop, label in enumerate(tail):
        for k in range(count):
            if hop == 0:
                waiting[k].wait_recv()
                add_in(k, steps - 1)
                copy = pltpu.make_async_copy(
                    held[k][steps - 1], outs[k].at[pl.ds(here, 1)], local.at[k]
                )
                copy.start()
                waiting[k] = copy
            for copy in inbox[k]:
                copy.wait_recv()
            inbox[k] = []
            shift = label[1] * (1 - 2 * my_bit(label))
            for n, offset in enumerate(list(known[k])):
                place = pl.ds(here + offset, 1)
                source = held[k][steps - 1] if n == 0 else outs[k].at[place]
                copy = send(source, outs[k].at[place], sems, k, steps + (1 << hop) - 1 + n, label)
                inbox[k].append(copy)
                open_sends.append(copy)
                known[k].append(offset + shift)
    waiting[count].wait_recv()
    before = sums[steps - 2]
    total[...] = before[...] + sums[steps - 1][...]
    for k in range(count):
        for copy in inbox[k]:
            copy.wait_recv()
        waiting[k].wait()
    for copy in open_sends:
        copy.wait_send()


def reduce_all(plan, grads, vector):
    steps = len(plan[0])
    reps = lax.axis_size("rep")
    vmem = pl.BlockSpec(memory_space=pltpu.VMEM)
    slots = pltpu.SemaphoreType.DMA((len(grads) + 1, steps + reps))
    scratch = []
    for grad in grads:
        scratch += [
            pltpu.VMEM((1 << (steps - 1 - step),) + grad.shape[1:], grad.dtype)
            for step in range(steps)
        ]
    scratch += [pltpu.VMEM(vector.shape, vector.dtype) for _ in range(steps)]
    return pl.pallas_call(
        functools.partial(reduce_kernel, plan, bits_of("rep")),
        in_specs=[vmem] * (len(grads) + 1),
        out_specs=[vmem] * (len(grads) + 1),
        out_shape=[jax.ShapeDtypeStruct((reps,) + g.shape[1:], g.dtype) for g in grads]
        + [jax.ShapeDtypeStruct(vector.shape, vector.dtype)],
        scratch_shapes=scratch + [slots, slots, pltpu.SemaphoreType.DMA((len(grads),))],
        compiler_params=pltpu.CompilerParams(
            collective_id=1, has_side_effects=True, vmem_limit_bytes=60 << 20
        ),
        name="reduce_grads",
    )(*grads, vector)


def to_order(array, order):
    labels = all_labels()
    rows = array.shape[0] >> len(labels)
    perm = [labels.index(label) for label in order] + [len(labels), len(labels) + 1]
    split = array.reshape((2,) * len(labels) + (rows, array.shape[1]))
    return split.transpose(perm).reshape((-1, rows, array.shape[1]))


def from_order(blocks, order):
    labels = all_labels()
    perm = [order.index(label) for label in labels] + [len(labels), len(labels) + 1]
    split = blocks.reshape((2,) * len(labels) + blocks.shape[1:])
    return split.transpose(perm).reshape((-1, blocks.shape[-1]))


def whole_lanes(array):
    return jnp.pad(array, ((0, 0), (0, -array.shape[1] % LANES)))


def my_rows(shard):
    count = shard.shape[0] // lax.axis_size("rep")
    return lax.dynamic_slice_in_dim(shard, lax.axis_index("rep") * count, count, 0)


SMALL = ("gain", "cw", "cb", "sb", "dl", "sk", "mg")


def core_kernel(names, *refs):
    r = Refs()
    at = 0
    for name, many in names:
        if many:
            setattr(r, name, list(refs[at : at + many]))
            at += many
        else:
            setattr(r, name, refs[at])
            at += 1
    r.ex = r.z
    stage_norm(r)
    for k in range(GROUP):
        stage_proj_x(r, k)
    stage_conv(r)
    stage_steps(r)
    stage_scan(r)
    for k in range(GROUP):
        stage_proj_z(r, k)
    stage_gate(r)
    stage_out(r)
    for k in range(GROUP):
        stage_grad_out(r, k)
    stage_gate_back(r)
    for k in range(GROUP):
        stage_grad_z(r, k)
    stage_scan_back(r)
    stage_conv_back(r)
    for k in range(GROUP):
        stage_grad_x(r, k)
    stage_grad_in(r)
    stage_norm_back(r)
    stage_vectors(r)


def run_core(count, hidden, cot, small, wx, wz, wo):
    total, wide = hidden.shape
    f32, bf16 = jnp.float32, jnp.bfloat16
    scratch = core_scratch(total, wide)
    vmem = pl.BlockSpec(memory_space=pltpu.VMEM)
    smem = pl.BlockSpec(memory_space=pltpu.SMEM)
    outs = [((total, wide), bf16), ((total, wide), f32), ((8, CONV_CH), f32)]
    outs += [(w.shape, bf16) for w in wx + wz + wo]
    names = [("count", 0), ("hidden", 0), ("cot", 0)] + [(name, 0) for name in SMALL]
    names += [("wx", GROUP), ("wz", GROUP), ("wo", GROUP)]
    names += [("block_out", 0), ("grad_in", 0), ("vec", 0)]
    names += [("gwx", GROUP), ("gwz", GROUP), ("gwo", GROUP)]
    names += [(name, 0) for name in scratch]
    inputs = [count, hidden, cot] + [small[name] for name in SMALL] + wx + wz + wo
    return pl.pallas_call(
        functools.partial(core_kernel, names),
        in_specs=[smem] + [vmem] * (len(inputs) - 1),
        out_specs=[vmem] * len(outs),
        out_shape=[jax.ShapeDtypeStruct(*out) for out in outs],
        scratch_shapes=[pltpu.VMEM(*item) for item in scratch.values()],
        compiler_params=pltpu.CompilerParams(vmem_limit_bytes=67043328),
        name="mixer_block",
    )(*inputs)


def lane_row(array):
    return jnp.pad(array, (0, LANES - array.shape[0])).reshape(1, LANES)


def cuts_of():
    wide = -(-(CONV_CH + NH) // (GROUP * LANES)) * LANES
    x_cuts = [slice(DI + k * wide, min(DI + (k + 1) * wide, PROJ)) for k in range(GROUP)]
    z_cuts = [slice(k * DI // GROUP, (k + 1) * DI // GROUP) for k in range(GROUP)]
    return x_cuts, z_cuts


def body(
    hidden_in, cotangent, lengths, norm_gain, in_weight, conv_weight, conv_bias,
    step_bias, decay_log, skip_weight, mix_gain, out_weight,
):
    assert lengths.shape[0] == 1 and hidden_in.shape[0] % QLEN == 0
    plan = orders()
    x_cuts, z_cuts = cuts_of()
    width = out_weight.shape[1] // GROUP
    out_columns = [slice(k * width, (k + 1) * width) for k in range(GROUP)]
    small = jnp.concatenate([norm_gain, conv_weight.reshape(-1), conv_bias, mix_gain])
    small = jnp.pad(small, (0, -small.size % 2048)).reshape(1, -1, LANES)
    in_rows, out_rows = my_rows(in_weight), my_rows(out_weight)
    pieces = [whole_lanes(in_rows[:, cut])[None] for cut in x_cuts + z_cuts]
    pieces += [out_rows[None, :, cut] for cut in out_columns]
    wide_plan = list(plan) * 3
    gathered = gather_all([bits_of("fsdp")] + wide_plan, [small] + pieces)
    full = [from_order(blocks, order) for blocks, order in zip(gathered[1:], wide_plan)]
    small = gathered[0].reshape(lax.axis_size("fsdp"), -1)
    groups = small.shape[0]
    ends = [norm_gain.size, conv_weight.size, conv_bias.size]
    cut_a, cut_b, cut_c = ends[0], ends[0] + ends[1], sum(ends)
    f32 = jnp.float32
    params = dict(
        gain=small[:, :cut_a].reshape(1, -1).astype(f32),
        cw=small[:, cut_a:cut_b]
        .reshape(groups, KCONV, -1)
        .transpose(1, 0, 2)
        .reshape(KCONV, -1)
        .astype(f32),
        cb=small[:, cut_b:cut_c].reshape(1, -1).astype(f32),
        mg=small[:, cut_c : cut_c + mix_gain.size].reshape(1, -1).astype(f32),
        sb=lane_row(step_bias),
        dl=lane_row(decay_log),
        sk=lane_row(skip_weight),
    )
    block_out, grad_in, vec, *grads = run_core(
        lengths, hidden_in, cotangent, params, full[:3], full[3:6], full[6:]
    )
    blocks = [to_order(part, order) for part, order in zip(grads, wide_plan)]
    *sums, vec = reduce_all(wide_plan, blocks, vec)
    sums = [part.reshape(-1, part.shape[-1]) for part in sums]
    g_in = jnp.concatenate(sums[3:6] + sums[:3], axis=1)[:, :PROJ].astype(f32)
    g_out = jnp.concatenate(sums[6:], axis=1).astype(f32)
    me = lax.axis_index("fsdp")

    def mine(array):
        count = array.shape[-1] // groups
        return lax.dynamic_slice_in_dim(array, me * count, count, array.ndim - 1)

    g_cw = mine(vec[:KCONV])
    g_cb = mine(vec[KCONV])
    g_mg = mine(vec[5, :DI])
    g_gain = mine(vec[6, : hidden_in.shape[1]])
    g_sb, g_dl, g_sk = (vec[7, k * LANES : k * LANES + NH] for k in range(3))
    return (block_out, grad_in, g_gain, g_in, g_cw, g_cb, g_sb, g_dl, g_sk, g_mg, g_out)


def solution(mesh):
    in_specs = (
        P(("fsdp", "rep"), None),
        P(("fsdp", "rep"), None),
        P(("fsdp", "rep")),
        P("fsdp"),
        P("fsdp", None),
        P(None, "fsdp"),
        P("fsdp"),
        P(),
        P(),
        P(),
        P("fsdp"),
        P("fsdp", None),
    )
    out_specs = (
        P(("fsdp", "rep"), None),
        P(("fsdp", "rep"), None),
        P("fsdp"),
        P("fsdp", None),
        P(None, "fsdp"),
        P("fsdp"),
        P(),
        P(),
        P(),
        P("fsdp"),
        P("fsdp", None),
    )
    return jax.shard_map(body, mesh=mesh, in_specs=in_specs, out_specs=out_specs, check_vma=False)
```

```python
import functools


import jax
import jax.numpy as jnp
from jax import lax
from jax.experimental import pallas as pl
from jax.experimental.pallas import tpu as pltpu
from jax.sharding import PartitionSpec as P

NH = 24
HD = 64
NS = 128
KCONV = 4
DI = 1536
CONV_CH = 1792
PROJ = 3352
LANES = 128
PAIR = LANES // HD

EPS = 1e-05
HIGH = lax.Precision.HIGHEST


def contract(left, right, left_dim, right_dim, precision=None):
    return lax.dot_general(
        left,
        right,
        (((left_dim,), (right_dim,)), ((), ())),
        precision=precision,
        preferred_element_type=jnp.float32,
    )


LOG2E = 1.4426950408889634
QLEN = 128
GROUP = 3


def split_hi_lo(value):
    high = value.astype(jnp.bfloat16)
    return high, (value - high.astype(jnp.float32)).astype(jnp.bfloat16)


def run_queue(i, count, queue):
    for n, item in enumerate(queue):
        pl.when(i == min(n, count - 1))(item)


def row_loop(total, size, step, queue=()):
    def one(i, carry):
        step(pl.multiple_of(i * size, size))
        run_queue(i, total // size, queue)
        return carry

    lax.fori_loop(0, total // size, one, 0)


def fold(value):
    return jnp.sum(value.reshape(-1, 8, value.shape[-1]), axis=0)


def head_expander(width):
    row = lax.broadcasted_iota(jnp.int32, (LANES, width), 0)
    col = lax.broadcasted_iota(jnp.int32, (LANES, width), 1)
    return jnp.where(row % HD == col // HD, 1.0, 0.0).astype(jnp.bfloat16)


def head_summer(width):
    row = lax.broadcasted_iota(jnp.int32, (width, LANES), 0)
    col = lax.broadcasted_iota(jnp.int32, (width, LANES), 1)
    return jnp.where(row // HD == col, 1.0, 0.0).astype(jnp.bfloat16)


def two_part(value):
    high = value.astype(jnp.bfloat16).astype(jnp.float32)
    low = pltpu.roll(value - high, HD, 1)
    lane = lax.broadcasted_iota(jnp.int32, value.shape, 1)
    return jnp.where(lane < HD, high, low).astype(jnp.bfloat16)


def spans_of(pieces):
    spans, at = [], 0
    for piece in pieces:
        spans.append(slice(at, at + piece.shape[1]))
        at += piece.shape[1]
    return spans


def stage_norm(r):
    total = r.hidden.shape[0]

    def step(at):
        rows = pl.ds(at, 64)
        h = r.hidden[rows, :].astype(jnp.float32)
        scale = lax.rsqrt(jnp.mean(h * h, axis=-1, keepdims=True) + EPS)
        r.nb[rows, :] = (h * scale * r.gain[...]).astype(jnp.bfloat16)

    row_loop(total, 64, step)
    r.nbt[...] = r.nb[...].T


def stage_consts(r):
    r.expand[...] = head_expander(DI)
    r.summer[...] = head_summer(DI)


def stage_proj_x(r, k):
    total = r.hidden.shape[0]
    r.raw[8 : 8 + total, spans_of(r.wx)[k]] = contract(r.nb[...], r.wx[k][...], 1, 0)


def stage_conv(r):
    total = r.hidden.shape[0]
    r.raw[0:8, :] = jnp.zeros((8, r.raw.shape[1]), jnp.float32)
    size, wide = 64, 256

    def step(at):
        for lanes in range(0, CONV_CH, wide):
            cols = slice(lanes, lanes + wide)
            block = r.raw[pl.ds(at, size + 8), cols]
            conv = jnp.zeros((size, wide), jnp.float32) + r.cb[:, cols]
            for k in range(KCONV):
                start = 8 - (KCONV - 1) + k
                conv = conv + r.cw[k : k + 1, cols] * block[start : start + size]
            sig = jax.nn.sigmoid(conv)
            act = conv * sig
            r.act[pl.ds(at, size), cols] = act
            r.dsil[pl.ds(at, size), cols] = sig + act * (1.0 - sig)

    row_loop(total, size, step)


def stage_steps(r):
    total = r.hidden.shape[0]
    lane = lax.broadcasted_iota(jnp.int32, (1, LANES), 1)
    rate = jnp.where(lane < NH, jnp.exp(r.dl[...]), 0.0)
    row = lax.broadcasted_iota(jnp.int32, (QLEN, QLEN), 0)
    col = lax.broadcasted_iota(jnp.int32, (QLEN, QLEN), 1)
    lower = jnp.where(row >= col, 1.0, 0.0)

    def step(at):
        rows = pl.ds(at, QLEN)
        pre = r.raw[pl.ds(at + 8, QLEN), CONV_CH : CONV_CH + LANES] + r.sb[...]
        dt = jnp.maximum(pre, 0.0) + jnp.log1p(jnp.exp(-jnp.abs(pre)))
        dt = jnp.where(lane < NH, dt, 0.0)
        r.dt[rows, :] = dt
        r.sgd[rows, :] = jax.nn.sigmoid(pre)
        cum = contract(lower, -dt * rate, 1, 0, lax.Precision.HIGHEST) * LOG2E
        r.cum[rows, :] = cum
        r.cumt[rows, :] = cum.T

    row_loop(total, QLEN, step)


def chunk_factors(r, rows):
    cum = r.cum[rows, :]
    last = cum[QLEN - 1 : QLEN, :]
    stack = jnp.concatenate(
        [two_part(r.dt[rows, :]), two_part(jnp.exp2(cum)), two_part(jnp.exp2(last - cum))], axis=0
    )
    half = DI // 2
    for side in range(2):
        cols = slice(side * half, (side + 1) * half)
        r.ex[0 : 3 * QLEN, cols] = contract(stack, r.expand[:, cols], 1, 0)


def halves(value):
    lane = lax.broadcasted_iota(jnp.int32, value.shape, 1)
    zero = jnp.zeros_like(value)
    return jnp.concatenate(
        [jnp.where(lane < HD, value, zero), jnp.where(lane >= HD, value, zero)], axis=0
    )


def stage_scan(r, queue=()):
    total = r.hidden.shape[0]
    row = lax.broadcasted_iota(jnp.int32, (QLEN, QLEN), 0)
    col = lax.broadcasted_iota(jnp.int32, (QLEN, QLEN), 1)
    r.state[...] = jnp.zeros_like(r.state)

    def step(at):
        rows = pl.ds(at, QLEN)
        keys = r.act[rows, DI : DI + NS]
        query = r.act[rows, DI + NS : DI + 2 * NS]
        score = jnp.where(row >= col, contract(query, keys, 1, 1, lax.Precision.HIGHEST), 0.0)
        query_b = query.astype(jnp.bfloat16)
        keys_t = keys.T.astype(jnp.bfloat16)
        chunk_factors(r, rows)
        r.states[rows, :] = r.state[...].astype(jnp.bfloat16)
        cum = r.cum[rows, :]
        cumt = r.cumt[rows, :]
        for p in range(NH // PAIR):
            cols = slice(p * LANES, (p + 1) * LANES)
            x = r.act[rows, cols]
            scaled_f = x * r.ex[0:QLEN, cols]
            scaled = scaled_f.astype(jnp.bfloat16)
            tail = (scaled_f * r.ex[2 * QLEN : 3 * QLEN, cols]).astype(jnp.bfloat16)
            parts = []
            for sub in range(PAIR):
                head = p * PAIR + sub
                spread = cum[:, head : head + 1] - cumt[head : head + 1, :]
                parts.append((score * jnp.exp2(jnp.minimum(spread, 0.0))).astype(jnp.bfloat16))
            inner = contract(jnp.concatenate(parts, axis=1), halves(scaled), 1, 0)
            lead = r.ex[QLEN : 2 * QLEN, cols]
            outer = contract(query_b, r.states[rows, cols], 1, 0)
            r.ysc[rows, cols] = inner + lead * outer
            r.state[:, cols] = lead[QLEN - 1 : QLEN, :] * r.state[:, cols] + contract(
                keys_t, tail, 1, 0
            )

    row_loop(total, QLEN, step, queue)


def stage_proj_z(r, k):
    r.z[:, spans_of(r.wz)[k]] = contract(r.nb[...], r.wz[k][...], 1, 0)


def stage_gate(r):
    total = r.hidden.shape[0]
    size = 16
    r.skx[...] = contract(two_part(jnp.broadcast_to(r.sk[...], (8, LANES))), r.expand[...], 1, 0)

    def step(at):
        rows = pl.ds(at, size)
        y = r.ysc[rows, :] + r.skx[0:1, :] * r.act[rows, 0:DI]
        z = r.z[rows, :]
        q = y * (z * jax.nn.sigmoid(z))
        scale = lax.rsqrt(jnp.mean(q * q, axis=-1, keepdims=True) + EPS)
        r.gb[rows, :] = (q * scale * r.mg[...]).astype(jnp.bfloat16)
        r.r2[rows, :] = jnp.broadcast_to(scale, (size, LANES))

    row_loop(total, size, step)


def live_rows(r, at, size):
    position = lax.broadcasted_iota(jnp.int32, (size, 1), 0) + at
    return jnp.where(position < r.count[0], 1.0, 0.0)


def stage_out(r):
    total, wide = r.hidden.shape

    def step(at):
        rows = pl.ds(at, 64)
        live = live_rows(r, at, 64)
        r.cl[rows, :] = (r.cot[rows, :].astype(jnp.float32) * live).astype(jnp.bfloat16)

    row_loop(total, 64, step)
    parts = len(r.wo)
    width = wide // parts
    for k in range(parts):
        cols = slice(k * width, (k + 1) * width)
        branch = contract(r.gb[...], r.wo[k][...], 1, 0)
        live = live_rows(r, 0, total)
        r.block_out[:, cols] = (r.hidden[:, cols].astype(jnp.float32) + live * branch).astype(
            jnp.bfloat16
        )
    block = 256
    for at in range(0, DI, block):
        sums = None
        for k in range(parts):
            cols = slice(k * width, (k + 1) * width)
            term = contract(r.cl[:, cols], r.wo[k][at : at + block, :], 1, 1)
            sums = term if sums is None else sums + term
        r.dy[:, at : at + block] = sums


def stage_grad_out(r, k):
    width = r.gwo[k].shape[1]
    part = contract(r.gb[...], r.cl[:, k * width : (k + 1) * width], 0, 0)
    r.gwo[k][...] = part.astype(jnp.bfloat16)


def stage_gate_back(r):
    total = r.hidden.shape[0]
    size = 16
    r.acc_mg[...] = jnp.zeros_like(r.acc_mg)
    r.acc_sk[...] = jnp.zeros_like(r.acc_sk)

    def step(at):
        rows = pl.ds(at, size)
        x = r.act[rows, 0:DI]
        y = r.ysc[rows, :] + r.skx[0:1, :] * x
        z = r.z[rows, :]
        sig = jax.nn.sigmoid(z)
        gate = z * sig
        q = y * gate
        scale = r.r2[rows, 0:1]
        dg = r.dy[rows, :]
        r.acc_mg[...] += fold(dg * q * scale)
        dn = dg * r.mg[...]
        mean = jnp.sum(dn * q, axis=-1, keepdims=True) * (1.0 / DI)
        dq = scale * (dn - q * (scale * scale * mean))
        dy = dq * gate
        r.dy[rows, :] = dy
        r.acc_sk[...] += fold(dy * x)
        r.dz[rows, :] = (dq * y * (sig + gate * (1.0 - sig))).astype(jnp.bfloat16)

    row_loop(total, size, step)


def stage_grad_z(r, k):
    part = contract(r.nbt[...], r.dz[:, spans_of(r.gwz)[k]], 1, 0)
    r.gwz[k][...] = part.astype(jnp.bfloat16)


def head_sums(r, values):
    parts = []
    for value in values:
        parts += list(split_hi_lo(value))
    sums = contract(jnp.concatenate(parts, axis=0), r.summer[...], 1, 0)
    out, at = [], 0
    for value in values:
        count = value.shape[0]
        out.append(sums[at : at + count] + sums[at + count : at + 2 * count])
        at += 2 * count
    return out


def stage_scan_back(r, queue=()):
    total = r.hidden.shape[0]
    chunks = total // QLEN
    row = lax.broadcasted_iota(jnp.int32, (QLEN, QLEN), 0)
    col = lax.broadcasted_iota(jnp.int32, (QLEN, QLEN), 1)
    upper = jnp.where(col >= row, 1.0, 0.0)
    lane = lax.broadcasted_iota(jnp.int32, (1, LANES), 1)
    rate = jnp.where(lane < NH, jnp.exp(r.dl[...]), 0.0)
    r.dstate[...] = jnp.zeros_like(r.dstate)
    r.acc_dl[...] = jnp.zeros_like(r.acc_dl)
    r.acc_sb[...] = jnp.zeros_like(r.acc_sb)

    def step(i, carry):
        at = pl.multiple_of((chunks - 1 - i) * QLEN, QLEN)
        rows = pl.ds(at, QLEN)
        keys = r.act[rows, DI : DI + NS]
        query = r.act[rows, DI + NS : DI + 2 * NS]
        score = jnp.where(col >= row, contract(keys, query, 1, 1, lax.Precision.HIGHEST), 0.0)
        keys_b = keys.astype(jnp.bfloat16)
        query_t = query.T.astype(jnp.bfloat16)
        chunk_factors(r, rows)
        cum = r.cum[rows, :]
        cumt = r.cumt[rows, :]
        r.dscore[...] = jnp.zeros_like(r.dscore)
        r.dkq[...] = jnp.zeros_like(r.dkq)
        for p in range(NH // PAIR):
            cols = slice(p * LANES, (p + 1) * LANES)
            dy = r.dy[rows, cols]
            dy_b = dy.astype(jnp.bfloat16)
            x = r.act[rows, cols]
            scaled_f = x * r.ex[0:QLEN, cols]
            scaled = scaled_f.astype(jnp.bfloat16)
            tail = (scaled_f * r.ex[2 * QLEN : 3 * QLEN, cols]).astype(jnp.bfloat16)
            lead = r.ex[QLEN : 2 * QLEN, cols]
            stacked = halves(dy_b)
            d_mixed = contract(scaled, stacked, 1, 1)
            parts = []
            gain = None
            for sub in range(PAIR):
                head = p * PAIR + sub
                spread = cumt[head : head + 1, :] - cum[:, head : head + 1]
                decay = jnp.exp2(jnp.minimum(spread, 0.0))
                term = d_mixed[:, sub * QLEN : (sub + 1) * QLEN] * decay
                gain = term if gain is None else gain + term
                parts.append((score * decay).astype(jnp.bfloat16))
            r.dscore[...] += gain
            d_state = r.dstate[:, cols]
            d_state_b = d_state.astype(jnp.bfloat16)
            d_scaled = contract(jnp.concatenate(parts, axis=1), stacked, 1, 0)
            d_outer = r.ex[2 * QLEN : 3 * QLEN, cols] * contract(keys_b, d_state_b, 1, 0)
            d_scaled = d_scaled + d_outer
            dy_lead = (dy * lead).astype(jnp.bfloat16)
            r.dkq[:, 0:NS] += contract(tail, d_state_b, 1, 1)
            r.dkq[:, NS : 2 * NS] += contract(dy_lead, r.states[rows, cols], 1, 1)
            kept = lead[QLEN - 1 : QLEN, :] * r.states[rows, cols].astype(jnp.float32)
            across = kept * d_state + scaled.astype(jnp.float32) * d_outer
            r.zrow[0:1, cols] = jnp.sum(across, axis=0, keepdims=True)
            r.dstate[:, cols] = lead[QLEN - 1 : QLEN, :] * d_state + contract(
                query_t, dy_lead, 1, 0
            )
            r.prod[0:QLEN, cols] = (
                dy_b.astype(jnp.float32) * r.ysc[rows, cols]
                - scaled.astype(jnp.float32) * d_scaled
            )
            r.prod[QLEN : 2 * QLEN, cols] = x * d_scaled
            dx = d_scaled * r.ex[0:QLEN, cols] + r.skx[0:1, cols] * dy
            r.act[rows, cols] = dx * r.dsil[rows, cols]
        dscore = jnp.where(col >= row, r.dscore[...], 0.0)
        d_keys = contract(dscore, query, 1, 0, lax.Precision.HIGHEST) + r.dkq[:, 0:NS]
        d_query = contract(dscore.T, keys, 1, 0, lax.Precision.HIGHEST) + r.dkq[:, NS : 2 * NS]
        both = jnp.concatenate([d_keys, d_query], axis=1)
        r.act[rows, DI:CONV_CH] = both * r.dsil[rows, DI:CONV_CH]
        flow, d_dt, across = head_sums(
            r, [r.prod[0:QLEN, :], r.prod[QLEN : 2 * QLEN, :], jnp.broadcast_to(r.zrow[0:1, :], (16, DI))]
        )
        da = contract(upper, flow, 1, 0, lax.Precision.HIGHEST) + across[0:1, :]
        dt = r.dt[rows, :]
        r.acc_dl[...] += fold(-da * dt * rate)
        d_pre = (d_dt - da * rate) * r.sgd[rows, :]
        d_pre = jnp.where(lane < NH, d_pre, 0.0)
        r.acc_sb[...] += fold(d_pre)
        r.dxb[rows, CONV_CH : CONV_CH + LANES] = d_pre.astype(jnp.bfloat16)
        rest = r.dxb.shape[1] - CONV_CH - LANES
        if rest:
            r.dxb[rows, CONV_CH + LANES :] = jnp.zeros((QLEN, rest), jnp.bfloat16)
        run_queue(i, chunks, queue)
        return carry

    lax.fori_loop(0, chunks, step, 0)


def stage_conv_back(r):
    total = r.hidden.shape[0]
    size, wide = 64, 256
    r.act[total : total + 8, :] = jnp.zeros((8, CONV_CH), jnp.float32)
    r.acc_cw[...] = jnp.zeros_like(r.acc_cw)

    def step(at):
        for lanes in range(0, CONV_CH, wide):
            cols = slice(lanes, lanes + wide)
            grads = r.act[pl.ds(at, size + 8), cols]
            inputs = r.raw[pl.ds(at, size + 8), cols]
            here = grads[0:size]
            total_in = None
            for k in range(KCONV):
                shift = KCONV - 1 - k
                term = r.cw[k : k + 1, cols] * grads[shift : shift + size]
                total_in = term if total_in is None else total_in + term
                start = 8 - (KCONV - 1) + k
                r.acc_cw[k * 8 : (k + 1) * 8, cols] += fold(here * inputs[start : start + size])
            r.acc_cw[KCONV * 8 : (KCONV + 1) * 8, cols] += fold(here)
            r.dxb[pl.ds(at, size), cols] = total_in.astype(jnp.bfloat16)

    row_loop(total, size, step)


def stage_grad_x(r, k):
    part = contract(r.nbt[...], r.dxb[:, spans_of(r.gwx)[k]], 1, 0)
    r.gwx[k][...] = part.astype(jnp.bfloat16)


def stage_grad_in(r, grads, weights, first):
    wide = r.hidden.shape[1]
    block = 256
    for at in range(0, wide, block):
        sums = None if first else r.grad_in[:, at : at + block]
        for span, weight in zip(spans_of(weights), weights):
            term = contract(grads[:, span], weight[at : at + block, :], 1, 1)
            sums = term if sums is None else sums + term
        r.grad_in[:, at : at + block] = sums


def stage_norm_back(r):
    total, wide = r.hidden.shape
    r.acc_gain[...] = jnp.zeros_like(r.acc_gain)

    def step(at):
        rows = pl.ds(at, 32)
        h = r.hidden[rows, :].astype(jnp.float32)
        scale = lax.rsqrt(jnp.mean(h * h, axis=-1, keepdims=True) + EPS)
        dn = r.grad_in[rows, :]
        r.acc_gain[...] += fold(dn * (h * scale))
        dn = dn * r.gain[...]
        mean = jnp.sum(dn * h, axis=-1, keepdims=True) * (1.0 / wide)
        r.grad_in[rows, :] = r.cot[rows, :].astype(jnp.float32) + scale * (
            dn - h * (scale * scale * mean)
        )

    row_loop(total, 32, step)


def stage_vectors(r):
    r.vec[...] = jnp.zeros_like(r.vec)
    for k in range(KCONV + 1):
        r.vec[k : k + 1, :] = jnp.sum(r.acc_cw[k * 8 : (k + 1) * 8, :], axis=0, keepdims=True)
    r.vec[5:6, 0:DI] = jnp.sum(r.acc_mg[...], axis=0, keepdims=True)
    wide = r.acc_gain.shape[1]
    r.vec[6:7, 0:wide] = jnp.sum(r.acc_gain[...], axis=0, keepdims=True)
    r.vec[7:8, 0:LANES] = jnp.sum(r.acc_sb[...], axis=0, keepdims=True)
    r.vec[7:8, LANES : 2 * LANES] = jnp.sum(r.acc_dl[...], axis=0, keepdims=True)
    sums = jnp.sum(r.acc_sk[...], axis=0, keepdims=True)
    (heads,) = head_sums(r, [jnp.broadcast_to(sums, (16, DI))])
    r.vec[7:8, 2 * LANES : 3 * LANES] = heads[0:1, :]


class Refs:
    pass


def core_scratch(total, wide, span):
    f32, bf16 = jnp.float32, jnp.bfloat16
    return dict(
        nb=((total, wide), bf16),
        nbt=((wide, total), bf16),
        expand=((LANES, DI), bf16),
        summer=((DI, LANES), bf16),
        raw=((total + 8, span), f32),
        act=((total + 8, CONV_CH), f32),
        dsil=((total, CONV_CH), f32),
        dt=((total, LANES), f32),
        sgd=((total, LANES), f32),
        cum=((total, LANES), f32),
        cumt=((total, LANES), f32),
        state=((NS, DI), f32),
        dstate=((NS, DI), f32),
        states=((total, DI), bf16),
        ysc=((total, DI), f32),
        z=((total, DI), f32),
        skx=((8, DI), f32),
        gb=((total, DI), bf16),
        r2=((total, LANES), f32),
        cl=((total, wide), bf16),
        dy=((total, DI), f32),
        dz=((total, DI), bf16),
        dxb=((total, span), bf16),
        dscore=((QLEN, QLEN), f32),
        dkq=((QLEN, 2 * NS), f32),
        zrow=((8, DI), f32),
        prod=((2 * QLEN, DI), f32),
        acc_mg=((8, DI), f32),
        acc_sk=((8, DI), f32),
        acc_dl=((8, LANES), f32),
        acc_sb=((8, LANES), f32),
        acc_cw=((8 * (KCONV + 1), CONV_CH), f32),
        acc_gain=((8, wide), f32),
    )


def bits_of(axis):
    size = lax.axis_size(axis)
    return [(axis, 1 << k) for k in reversed(range(size.bit_length() - 1))]


def all_labels():
    return bits_of("fsdp") + bits_of("rep")


def my_bit(label):
    return (lax.axis_index(label[0]) // label[1]) % 2


def partner(label):
    ids = {name: lax.axis_index(name) for name in ("fsdp", "rep")}
    ids[label[0]] = ids[label[0]] + label[1] * (1 - 2 * my_bit(label))
    return (ids["fsdp"], ids["rep"])


def greet(labels):
    barrier = pltpu.get_barrier_semaphore()
    for label in labels:
        pl.semaphore_signal(
            barrier, inc=1, device_id=partner(label), device_id_type=pl.DeviceIdType.MESH
        )
    pl.semaphore_wait(barrier, len(labels))


def send(source, target, sems, stream, slot, label):
    copy = pltpu.make_async_remote_copy(
        src_ref=source,
        dst_ref=target,
        send_sem=sems[0].at[stream, slot],
        recv_sem=sems[1].at[stream, slot],
        device_id=partner(label),
        device_id_type=pl.DeviceIdType.MESH,
    )
    copy.start()
    return copy


def orders():
    fsdp, rep = bits_of("fsdp"), bits_of("rep")
    near, wide = fsdp[-1:], fsdp[:-1]
    mid, far = wide[-1:], wide[:-1]
    core, row = rep[-1:], rep[:-1]
    return (
        core + row + near + mid + far,
        core + near + mid + row + far,
        core + mid + row + near + far,
    )


def position(order):
    place = 0
    for label in order:
        place = place * 2 + my_bit(label)
    return place


def gather_kernel(plan, *refs):
    count = len(plan)
    ins, outs = refs[:count], refs[count : 2 * count]
    sems, local = refs[2 * count : 2 * count + 2], refs[2 * count + 2]
    greet(all_labels())
    steps = max(len(order) for order in plan)
    open_sends, waiting, locals_ = [], {}, []
    for k in range(count):
        copy = pltpu.make_async_copy(ins[k], outs[k].at[pl.ds(position(plan[k]), 1)], local.at[k])
        copy.start()
        locals_.append(copy)
    for step in range(steps):
        for k, order in enumerate(plan):
            if step >= len(order):
                continue
            size = 1 << step
            start = position(order) // size * size
            if step == 0:
                source = ins[k]
            else:
                if step == 1:
                    locals_[k].wait()
                waiting[k].wait_recv()
                source = outs[k].at[pl.ds(start, size)]
            label = order[len(order) - 1 - step]
            copy = send(source, outs[k].at[pl.ds(start, size)], sems, k, step, label)
            waiting[k] = copy
            open_sends.append(copy)
    for k in range(count):
        waiting[k].wait_recv()
        if len(plan[k]) < 2:
            locals_[k].wait()
    for copy in open_sends:
        copy.wait_send()


def gather_all(plan, pieces):
    steps = max(len(order) for order in plan)
    vmem = pl.BlockSpec(memory_space=pltpu.VMEM)
    return pl.pallas_call(
        functools.partial(gather_kernel, plan),
        in_specs=[vmem] * len(pieces),
        out_specs=[vmem] * len(pieces),
        out_shape=[
            jax.ShapeDtypeStruct((1 << len(order),) + piece.shape[1:], piece.dtype)
            for order, piece in zip(plan, pieces)
        ],
        scratch_shapes=[
            pltpu.SemaphoreType.DMA((len(pieces), steps)),
            pltpu.SemaphoreType.DMA((len(pieces), steps)),
            pltpu.SemaphoreType.DMA((len(pieces),)),
        ],
        compiler_params=pltpu.CompilerParams(
            collective_id=0, has_side_effects=True, vmem_limit_bytes=60 << 20
        ),
        name="gather_weights",
    )(*pieces)


def reduce_kernel(plan, tail, *refs):
    count = len(plan)
    steps = len(plan[0])
    grads, vector = refs[:count], refs[count]
    outs, total = refs[count + 1 : 2 * count + 1], refs[2 * count + 1]
    at = 2 * count + 2
    held = [refs[at + k * steps : at + (k + 1) * steps] for k in range(count)]
    at += count * steps
    sums = refs[at : at + steps]
    sems, local = refs[at + steps : at + steps + 2], refs[at + steps + 2]
    labels = all_labels()
    greet(labels)
    open_sends, waiting = [], {}
    vector_order = labels[::-1]

    def source_of(k, step):
        return grads[k] if step == 0 else held[k][step - 1]

    def add_in(k, step):
        size = 1 << (steps - 1 - step)
        base = source_of(k, step)
        target = held[k][step]
        start = my_bit(plan[k][step]) * size

        def one(i, carry):
            left = base[start + i].astype(jnp.float32)
            target[i] = (left + target[i].astype(jnp.float32)).astype(target.dtype)
            return carry

        lax.fori_loop(0, size, one, 0)

    for step in range(steps):
        for k in range(count):
            if step > 0:
                waiting[k].wait_recv()
                add_in(k, step - 1)
            label = plan[k][step]
            size = 1 << (steps - 1 - step)
            away = source_of(k, step).at[pl.ds((1 - my_bit(label)) * size, size)]
            waiting[k] = send(away, held[k][step], sems, k, step, label)
            open_sends.append(waiting[k])
        if step > 0:
            waiting[count].wait_recv()
            before = vector if step == 1 else sums[step - 2]
            sums[step - 1][...] = before[...] + sums[step - 1][...]
        now = vector if step == 0 else sums[step - 1]
        waiting[count] = send(now, sums[step], sems, count, step, vector_order[step])
        open_sends.append(waiting[count])

    here = lax.axis_index("rep")
    known = {k: [0] for k in range(count)}
    inbox = {k: [] for k in range(count)}
    for hop, label in enumerate(tail):
        for k in range(count):
            if hop == 0:
                waiting[k].wait_recv()
                add_in(k, steps - 1)
                copy = pltpu.make_async_copy(
                    held[k][steps - 1], outs[k].at[pl.ds(here, 1)], local.at[k]
                )
                copy.start()
                waiting[k] = copy
            for copy in inbox[k]:
                copy.wait_recv()
            inbox[k] = []
            shift = label[1] * (1 - 2 * my_bit(label))
            for n, offset in enumerate(list(known[k])):
                place = pl.ds(here + offset, 1)
                source = held[k][steps - 1] if n == 0 else outs[k].at[place]
                copy = send(source, outs[k].at[place], sems, k, steps + (1 << hop) - 1 + n, label)
                inbox[k].append(copy)
                open_sends.append(copy)
                known[k].append(offset + shift)
    waiting[count].wait_recv()
    before = sums[steps - 2]
    total[...] = before[...] + sums[steps - 1][...]
    for k in range(count):
        for copy in inbox[k]:
            copy.wait_recv()
        waiting[k].wait()
    for copy in open_sends:
        copy.wait_send()


def reduce_all(plan, grads, vector):
    steps = len(plan[0])
    reps = lax.axis_size("rep")
    vmem = pl.BlockSpec(memory_space=pltpu.VMEM)
    slots = pltpu.SemaphoreType.DMA((len(grads) + 1, steps + reps))
    scratch = []
    for grad in grads:
        scratch += [
            pltpu.VMEM((1 << (steps - 1 - step),) + grad.shape[1:], grad.dtype)
            for step in range(steps)
        ]
    scratch += [pltpu.VMEM(vector.shape, vector.dtype) for _ in range(steps)]
    return pl.pallas_call(
        functools.partial(reduce_kernel, plan, bits_of("rep")),
        in_specs=[vmem] * (len(grads) + 1),
        out_specs=[vmem] * (len(grads) + 1),
        out_shape=[jax.ShapeDtypeStruct((reps,) + g.shape[1:], g.dtype) for g in grads]
        + [jax.ShapeDtypeStruct(vector.shape, vector.dtype)],
        scratch_shapes=scratch + [slots, slots, pltpu.SemaphoreType.DMA((len(grads),))],
        compiler_params=pltpu.CompilerParams(
            collective_id=1, has_side_effects=True, vmem_limit_bytes=60 << 20
        ),
        name="reduce_grads",
    )(*grads, vector)


def to_order(array, order):
    labels = all_labels()
    rows = array.shape[0] >> len(labels)
    perm = [labels.index(label) for label in order] + [len(labels), len(labels) + 1]
    split = array.reshape((2,) * len(labels) + (rows, array.shape[1]))
    return split.transpose(perm).reshape((-1, rows, array.shape[1]))


def from_order(blocks, order):
    labels = all_labels()
    perm = [order.index(label) for label in labels] + [len(labels), len(labels) + 1]
    split = blocks.reshape((2,) * len(labels) + blocks.shape[1:])
    return split.transpose(perm).reshape((-1, blocks.shape[-1]))


def whole_lanes(array):
    return jnp.pad(array, ((0, 0), (0, -array.shape[1] % LANES)))


def my_rows(shard):
    count = shard.shape[0] // lax.axis_size("rep")
    return lax.dynamic_slice_in_dim(shard, lax.axis_index("rep") * count, count, 0)


SMALL = ("gain", "cw", "cb", "sb", "dl", "sk", "mg")


def core_kernel(names, *refs):
    r = Refs()
    at = 0
    for name, many in names:
        if many:
            setattr(r, name, list(refs[at : at + many]))
            at += many
        else:
            setattr(r, name, refs[at])
            at += 1
    r.ex = r.z
    stage_consts(r)
    stage_norm(r)
    for k in range(GROUP):
        stage_proj_x(r, k)
    stage_conv(r)
    stage_steps(r)
    stage_scan(r)
    for k in range(GROUP):
        stage_proj_z(r, k)
    stage_gate(r)
    stage_out(r)
    for k in range(GROUP):
        stage_grad_out(r, k)
    stage_gate_back(r)
    for k in range(GROUP):
        stage_grad_z(r, k)
    stage_scan_back(r)
    stage_conv_back(r)
    for k in range(GROUP):
        stage_grad_x(r, k)
    stage_grad_in(r, r.dz, r.wz, True)
    stage_grad_in(r, r.dxb, r.wx, False)
    stage_norm_back(r)
    stage_vectors(r)


def run_core(count, hidden, cot, small, wx, wz, wo):
    total, wide = hidden.shape
    f32, bf16 = jnp.float32, jnp.bfloat16
    scratch = core_scratch(total, wide, sum(w.shape[1] for w in wx))
    vmem = pl.BlockSpec(memory_space=pltpu.VMEM)
    smem = pl.BlockSpec(memory_space=pltpu.SMEM)
    outs = [((total, wide), bf16), ((total, wide), f32), ((8, CONV_CH), f32)]
    outs += [(w.shape, bf16) for w in wx + wz + wo]
    names = [("count", 0), ("hidden", 0), ("cot", 0)] + [(name, 0) for name in SMALL]
    names += [("wx", GROUP), ("wz", GROUP), ("wo", GROUP)]
    names += [("block_out", 0), ("grad_in", 0), ("vec", 0)]
    names += [("gwx", GROUP), ("gwz", GROUP), ("gwo", GROUP)]
    names += [(name, 0) for name in scratch]
    inputs = [count, hidden, cot] + [small[name] for name in SMALL] + wx + wz + wo
    return pl.pallas_call(
        functools.partial(core_kernel, names),
        in_specs=[smem] + [vmem] * (len(inputs) - 1),
        out_specs=[vmem] * len(outs),
        out_shape=[jax.ShapeDtypeStruct(*out) for out in outs],
        scratch_shapes=[pltpu.VMEM(*item) for item in scratch.values()],
        compiler_params=pltpu.CompilerParams(vmem_limit_bytes=67043328),
        name="mixer_block",
    )(*inputs)


def lane_row(array):
    return jnp.pad(array, (0, LANES - array.shape[0])).reshape(1, LANES)


def cuts_of():
    wide = -(-(CONV_CH + NH) // (GROUP * LANES)) * LANES
    x_cuts = [slice(DI + k * wide, min(DI + (k + 1) * wide, PROJ)) for k in range(GROUP)]
    z_cuts = [slice(k * DI // GROUP, (k + 1) * DI // GROUP) for k in range(GROUP)]
    return x_cuts, z_cuts


def body(
    hidden_in, cotangent, lengths, norm_gain, in_weight, conv_weight, conv_bias,
    step_bias, decay_log, skip_weight, mix_gain, out_weight,
):
    assert lengths.shape[0] == 1 and hidden_in.shape[0] % QLEN == 0
    plan = orders()
    x_cuts, z_cuts = cuts_of()
    width = out_weight.shape[1] // GROUP
    out_columns = [slice(k * width, (k + 1) * width) for k in range(GROUP)]
    small = jnp.concatenate([norm_gain, conv_weight.reshape(-1), conv_bias, mix_gain])
    small = jnp.pad(small, (0, -small.size % 2048)).reshape(1, -1, LANES)
    in_rows, out_rows = my_rows(in_weight), my_rows(out_weight)
    pieces = [whole_lanes(in_rows[:, cut])[None] for cut in x_cuts + z_cuts]
    pieces += [out_rows[None, :, cut] for cut in out_columns]
    wide_plan = list(plan) * 3
    gathered = gather_all([bits_of("fsdp")] + wide_plan, [small] + pieces)
    full = [from_order(blocks, order) for blocks, order in zip(gathered[1:], wide_plan)]
    small = gathered[0].reshape(lax.axis_size("fsdp"), -1)
    groups = small.shape[0]
    ends = [norm_gain.size, conv_weight.size, conv_bias.size]
    cut_a, cut_b, cut_c = ends[0], ends[0] + ends[1], sum(ends)
    f32 = jnp.float32
    params = dict(
        gain=small[:, :cut_a].reshape(1, -1).astype(f32),
        cw=small[:, cut_a:cut_b]
        .reshape(groups, KCONV, -1)
        .transpose(1, 0, 2)
        .reshape(KCONV, -1)
        .astype(f32),
        cb=small[:, cut_b:cut_c].reshape(1, -1).astype(f32),
        mg=small[:, cut_c : cut_c + mix_gain.size].reshape(1, -1).astype(f32),
        sb=lane_row(step_bias),
        dl=lane_row(decay_log),
        sk=lane_row(skip_weight),
    )
    block_out, grad_in, vec, *grads = run_core(
        lengths, hidden_in, cotangent, params, full[:3], full[3:6], full[6:]
    )
    blocks = [to_order(part, order) for part, order in zip(grads, wide_plan)]
    *sums, vec = reduce_all(wide_plan, blocks, vec)
    sums = [part.reshape(-1, part.shape[-1]) for part in sums]
    g_in = jnp.concatenate(sums[3:6] + sums[:3], axis=1)[:, :PROJ].astype(f32)
    g_out = jnp.concatenate(sums[6:], axis=1).astype(f32)
    me = lax.axis_index("fsdp")

    def mine(array):
        count = array.shape[-1] // groups
        return lax.dynamic_slice_in_dim(array, me * count, count, array.ndim - 1)

    g_cw = mine(vec[:KCONV])
    g_cb = mine(vec[KCONV])
    g_mg = mine(vec[5, :DI])
    g_gain = mine(vec[6, : hidden_in.shape[1]])
    g_sb, g_dl, g_sk = (vec[7, k * LANES : k * LANES + NH] for k in range(3))
    return (block_out, grad_in, g_gain, g_in, g_cw, g_cb, g_sb, g_dl, g_sk, g_mg, g_out)


class Plan:
    def __init__(self, labels):
        self.labels = labels

    def region(self, ref, free, fixed=()):
        fixed = dict(fixed)
        index = []
        for label in self.labels:
            if label in fixed:
                index.append(pl.ds(fixed[label], 1))
            elif label in free:
                index.append(slice(None))
            else:
                index.append(pl.ds(my_bit(label), 1))
        return ref.at[tuple(index)]

    def own(self, ref):
        return ref.at[tuple(my_bit(label) for label in self.labels)]


class Spread:
    def __init__(self, labels, order, ref, sems, stream):
        self.plan, self.order, self.ref = Plan(labels), order, ref
        self.sems, self.stream = sems, stream

    def copy(self, step):
        done = self.order[len(self.order) - step :]
        label = self.order[len(self.order) - 1 - step]
        part = self.plan.region(self.ref, done)
        return pltpu.make_async_remote_copy(
            src_ref=part,
            dst_ref=part,
            send_sem=self.sems[0].at[self.stream, step],
            recv_sem=self.sems[1].at[self.stream, step],
            device_id=partner(label),
            device_id_type=pl.DeviceIdType.MESH,
        )

    def tick(self, step):
        if step > 0:
            self.copy(step - 1).wait_recv()
        if step < len(self.order):
            self.copy(step).start()

    def drain(self):
        for step in range(len(self.order)):
            self.copy(step).wait_send()


class Merge:
    def __init__(self, labels, order, ref, held, tail, sems, stream):
        spots = [label for label in labels if label[0] == "rep"]
        self.plan, self.order, self.ref, self.held = Plan(labels), order, ref, held
        self.sems, self.stream = sems, stream
        self.tail = Spread(spots, bits_of("rep"), tail, sems, stream + 1)

    def source(self, step):
        return self.ref if step == 0 else self.held[step - 1]

    def index(self, step, bit, rest):
        spots = []
        for label in self.plan.labels:
            if label in self.order[:step]:
                spots.append(0)
            elif label == self.order[step]:
                spots.append(bit)
            else:
                spots.append(rest[label])
        return tuple(spots)

    def copy(self, step):
        label = self.order[step]
        spots = []
        for name in self.plan.labels:
            spots.append(pl.ds(1 - my_bit(name), 1) if name == label else slice(None))
        return pltpu.make_async_remote_copy(
            src_ref=self.source(step).at[tuple(spots)],
            dst_ref=self.held[step],
            send_sem=self.sems[0].at[self.stream, step],
            recv_sem=self.sems[1].at[self.stream, step],
            device_id=partner(label),
            device_id_type=pl.DeviceIdType.MESH,
        )

    def add(self, step):
        label = self.order[step]
        free = [name for name in self.plan.labels if name not in self.order[: step + 1]]
        base, target = self.source(step), self.held[step]
        for number in range(1 << len(free)):
            rest = {name: (number >> place) % 2 for place, name in enumerate(free)}
            left = base[self.index(step, my_bit(label), rest)].astype(jnp.float32)
            spot = self.index(step, 0, rest)
            total = left + target[spot].astype(jnp.float32)
            target[spot] = total.astype(target.dtype)

    def tick(self, step):
        steps = len(self.order)
        if 0 < step <= steps:
            self.copy(step - 1).wait_recv()
            self.add(step - 1)
        if step < steps:
            self.copy(step).start()
            return
        if step == steps:
            spot = tuple(0 for _ in self.plan.labels)
            self.tail.plan.own(self.tail.ref)[...] = self.held[steps - 1][spot]
        self.tail.tick(step - steps)

    def last(self):
        return len(self.order) + len(self.tail.order)

    def drain(self):
        for step in range(len(self.order)):
            self.copy(step).wait_send()
        self.tail.drain()


class Total:
    def __init__(self, order, ref, held, sems, stream):
        self.order, self.ref, self.held = order, ref, held
        self.sems, self.stream = sems, stream

    def copy(self, step):
        return pltpu.make_async_remote_copy(
            src_ref=self.ref if step == 0 else self.held[step - 1],
            dst_ref=self.held[step],
            send_sem=self.sems[0].at[self.stream, step],
            recv_sem=self.sems[1].at[self.stream, step],
            device_id=partner(self.order[step]),
            device_id_type=pl.DeviceIdType.MESH,
        )

    def tick(self, step):
        if step > 0:
            self.copy(step - 1).wait_recv()
            before = self.ref if step == 1 else self.held[step - 2]
            self.held[step - 1][...] = before[...] + self.held[step - 1][...]
        if step < len(self.order):
            self.copy(step).start()

    def drain(self):
        for step in range(len(self.order)):
            self.copy(step).wait_send()


def side_widths():
    blocks = -(-(CONV_CH + NH) // (2 * LANES))
    cuts = [(blocks * k + GROUP - 1) // GROUP for k in range(GROUP + 1)]
    return [(cuts[k + 1] - cuts[k]) * LANES for k in range(GROUP)]


def side_labels():
    rep = bits_of("rep")
    return rep[-1:] + bits_of("fsdp") + rep[:-1]


def sides(refs):
    out = []
    for ref in refs:
        both = ref.reshape((2, _count(ref.shape[1:-1]), ref.shape[-1]))
        out += [both.at[0], both.at[1]]
    return out


def flat(ref):
    return ref.reshape((_count(ref.shape[:-1]), ref.shape[-1]))


def _count(shape):
    count = 1
    for size in shape:
        count *= size
    return count


def unpack_small(r, groups):
    blocks = r.small.reshape((groups, 16, 2 * LANES))
    size_cw, size_mg, size_gain = (item // groups for item in (CONV_CH, DI, r.hidden.shape[1]))
    pieces = [blocks[g] for g in range(groups)]
    r.cw[...] = jnp.concatenate([piece[0:8, :size_cw] for piece in pieces], axis=1)
    r.mg[...] = jnp.concatenate([piece[5:6, :size_mg] for piece in pieces], axis=1)
    r.gain[...] = jnp.concatenate([piece[6:7, :size_gain] for piece in pieces], axis=1)
    r.cb = r.cw.at[4:5, :]
    r.sb = r.small0.at[8:9, 0:LANES]
    r.dl = r.small0.at[9:10, 0:LANES]
    r.sk = r.small0.at[10:11, 0:LANES]


def finish_weights(r):
    rows = r.g_in.shape[0]
    at = 0
    for tail in r.tz + r.tx:
        wide = tail.shape[-1]
        for side in range(2):
            value = tail[side].astype(jnp.float32).reshape(rows, wide)
            stop = min(at + wide, PROJ)
            r.g_in[:, at:stop] = value[:, : stop - at]
            at = stop
    for k in range(GROUP):
        wide = r.to[k].shape[-1]
        r.g_out[:, k * wide : (k + 1) * wide] = (
            r.to[k][...].astype(jnp.float32).reshape(r.g_out.shape[0], wide)
        )


def finish_vectors(r, groups):
    me = lax.axis_index("fsdp")
    total = r.vheld[-1][...]
    full = total.shape[1]

    def mine(first, last, whole, out):
        count = whole // groups
        turned = pltpu.roll(total, (full - me * count) % full, 1)
        out[...] = turned[first:last, :count]

    mine(0, KCONV, CONV_CH, r.g_cw)
    mine(KCONV, KCONV + 1, CONV_CH, r.g_cb)
    mine(5, 6, DI, r.g_mg)
    mine(6, 7, r.hidden.shape[1], r.g_gain)
    for k, out in enumerate((r.g_sb, r.g_dl, r.g_sk)):
        out[...] = total[7:8, k * LANES : k * LANES + NH]


def fused_kernel(names, *refs):
    r = Refs()
    at = 0
    for name, many in names:
        if many:
            setattr(r, name, list(refs[at : at + many]))
            at += many
        else:
            setattr(r, name, refs[at])
            at += 1
    r.ex = r.z
    labels = all_labels()
    plan = orders()
    groups = lax.axis_size("fsdp")
    steps = len(labels)
    sems = (r.send, r.recv)
    side_first = side_labels()

    small = Spread(bits_of("fsdp"), bits_of("fsdp"), r.small, sems, 0)
    xs = [Spread(side_first, plan[k], r.bx[k], sems, 1 + k) for k in range(GROUP)]
    zs = [Spread(side_first, plan[k], r.bz[k], sems, 1 + GROUP + k) for k in range(GROUP)]
    os = [Spread(labels, plan[k], r.bo[k], sems, 1 + 2 * GROUP + k) for k in range(GROUP)]
    base = 1 + 3 * GROUP

    def merges(names_of, refs_of, helds, tails, offset):
        return [
            Merge(
                names_of, plan[k], refs_of[k], helds[k * steps : (k + 1) * steps], tails[k],
                sems, base + 2 * (offset + k),
            )
            for k in range(GROUP)
        ]

    mo = merges(labels, r.bo, r.ho, r.to, 0)
    mz = merges(side_first, r.bz, r.hz, r.tz, GROUP)
    mx = merges(side_first, r.bg, r.hx, r.tx, 2 * GROUP)
    total = Total(labels[::-1], r.vec, r.vheld, sems, base + 6 * GROUP)

    local = [pltpu.make_async_copy(r.small0, small.plan.own(r.small), r.local.at[0])]
    side = my_bit(side_first[0])
    rows = r.bz[0].shape[-2]
    here = pl.ds(pl.multiple_of(lax.axis_index("rep") // 2 * rows, 16), rows)
    at = 0
    for piece in zs + xs:
        wide = piece.ref.shape[-1]
        lanes = pl.ds(pl.multiple_of(at + side * wide, LANES), wide)
        local.append((piece, r.in_rows.at[here, lanes]))
        at += 2 * wide
    rows = r.bo[0].shape[-2]
    here = pl.ds(pl.multiple_of(lax.axis_index("rep") * rows, 16), rows)
    width = r.bo[0].shape[-1]
    for k in range(GROUP):
        local.append((os[k], r.out_rows.at[here, k * width : (k + 1) * width]))
    for n in range(1, len(local)):
        piece, source = local[n]
        local[n] = pltpu.make_async_copy(source, piece.plan.own(piece.ref), r.local.at[n])
    for copy in local:
        copy.start()
    greet(labels)
    for copy in local:
        copy.wait()

    def all_tick(pieces, step):
        for piece in pieces:
            piece.tick(step)

    r.wx, r.wz, r.gwx = sides(r.bx), sides(r.bz), sides(r.bg)
    r.wo = [flat(ref) for ref in r.bo]
    r.gwz, r.gwo = r.wz, r.wo

    fast = len(small.order)
    small.tick(0)
    all_tick(xs, 0)
    stage_consts(r)
    for step in range(1, fast + 1):
        small.tick(step)
        all_tick(xs, step)
    unpack_small(r, groups)
    stage_norm(r)
    for step in range(fast + 1, steps):
        all_tick(xs, step)
    all_tick(zs, 0)
    for k in range(GROUP):
        xs[k].tick(steps)
        stage_proj_x(r, 2 * k)
        stage_proj_x(r, 2 * k + 1)
    all_tick(zs, 1)
    stage_conv(r)
    all_tick(zs, 2)
    all_tick(os, 0)
    stage_steps(r)
    queue = [lambda s=s: all_tick(zs, s) for s in range(3, steps + 1)]
    queue += [lambda s=s: all_tick(os, s) for s in range(1, 2)]
    stage_scan(r, queue)
    for k in range(GROUP):
        stage_proj_z(r, 2 * k)
        stage_proj_z(r, 2 * k + 1)
        if 2 + k < steps:
            all_tick(os, 2 + k)
    stage_gate(r)
    for step in range(2 + GROUP, steps + 1):
        all_tick(os, step)
    stage_out(r)
    for piece in os + zs:
        piece.drain()
    for k in range(GROUP):
        stage_grad_out(r, k)
        mo[k].tick(0)
    stage_gate_back(r)
    all_tick(mo, 1)
    stage_grad_in(r, r.dz, r.wz, True)
    for k in range(GROUP):
        stage_grad_z(r, 2 * k)
        stage_grad_z(r, 2 * k + 1)
        mz[k].tick(0)
    all_tick(mo, 2)
    queue = []

    def both(s):
        all_tick(mz, s - 2)
        all_tick(mo, s)

    for s in range(3, 7):
        queue.append(lambda s=s: both(s))
    stage_scan_back(r, queue)
    last = mx[0].last()
    both(7)
    stage_conv_back(r)
    for k in range(GROUP):
        stage_grad_x(r, 2 * k)
        stage_grad_x(r, 2 * k + 1)
        mx[k].tick(0)
    all_tick(mz, 6)
    stage_grad_in(r, r.dxb, r.wx, False)
    all_tick(mz, 7)
    all_tick(mx, 1)
    stage_norm_back(r)
    stage_vectors(r)
    total.tick(0)
    for step in range(2, last + 1):
        all_tick(mx, step)
        if step - 1 <= steps:
            total.tick(step - 1)
    for step in range(last, steps + 1):
        total.tick(step)
    finish_weights(r)
    finish_vectors(r, groups)
    small.drain()
    for piece in xs + mo + mz + mx:
        piece.drain()
    total.drain()


def run_fused(count, hidden, cot, small0, in_rows, out_rows, in_shard, out_shard):
    total, wide = hidden.shape
    f32, bf16 = jnp.float32, jnp.bfloat16
    groups, reps = lax.axis_size("fsdp"), lax.axis_size("rep")
    labels, plan = all_labels(), orders()
    steps = len(labels)
    widths = side_widths()
    scratch = core_scratch(total, wide, 2 * sum(widths))
    nd = (2,) * steps
    ni, no = in_rows.shape[0] * 2 // reps, out_rows.shape[0] // reps
    wo = out_rows.shape[1] // GROUP
    wz = DI // (2 * GROUP)
    rep_bits = (2,) * len(bits_of("rep"))
    side_first = side_labels()
    groups_of = [
        ("x", ni, widths, side_first), ("z", ni, [wz] * GROUP, side_first),
        ("o", no, [wo] * GROUP, labels),
    ]
    buffers = [("small", [((2,) * len(bits_of("fsdp")) + small0.shape, f32)])]
    for name, rows, cols, order in groups_of:
        whole = [(nd + (rows, col), bf16) for col in cols]
        buffers.append(("b" + name, whole))
        if name == "x":
            buffers.append(("bg", whole))
        held = []
        for k in range(GROUP):
            for step in range(steps):
                gone = plan[k][: step + 1]
                kept = tuple(1 if n in gone else 2 for n in order)
                held.append((kept + (rows, cols[k]), bf16))
        buffers.append(("h" + name, held))
        buffers.append(("t" + name, [(rep_bits + (rows, col), bf16) for col in cols]))
    buffers.append(("vec", [((8, CONV_CH), f32)]))
    buffers.append(("vheld", [((8, CONV_CH), f32)] * steps))
    buffers.append(("cw", [((8, CONV_CH), f32)]))
    buffers.append(("mg", [((1, DI), f32)]))
    buffers.append(("gain", [((1, wide), f32)]))
    buffers += [(name, [item]) for name, item in scratch.items()]
    outs = [
        ("block_out", (total, wide), bf16),
        ("grad_in", (total, wide), f32),
        ("g_gain", (1, wide // groups), f32),
        ("g_in", in_shard, f32),
        ("g_cw", (KCONV, CONV_CH // groups), f32),
        ("g_cb", (1, CONV_CH // groups), f32),
        ("g_sb", (1, NH), f32),
        ("g_dl", (1, NH), f32),
        ("g_sk", (1, NH), f32),
        ("g_mg", (1, DI // groups), f32),
        ("g_out", out_shard, f32),
    ]
    names = [(n, 0) for n in ("count", "hidden", "cot", "small0", "in_rows", "out_rows")]
    names += [(out[0], 0) for out in outs]
    single = ("small", "vec", "cw", "mg", "gain") + tuple(scratch)
    shapes = []
    for name, items in buffers:
        names.append((name, 0 if name in single else len(items)))
        shapes += [pltpu.VMEM(*item) for item in items]
    names += [("send", 0), ("recv", 0), ("local", 0)]
    streams = 2 + 9 * GROUP
    slots = pltpu.SemaphoreType.DMA((streams, steps))
    shapes += [slots, slots, pltpu.SemaphoreType.DMA((1 + 3 * GROUP,))]
    vmem = pl.BlockSpec(memory_space=pltpu.VMEM)
    smem = pl.BlockSpec(memory_space=pltpu.SMEM)
    return pl.pallas_call(
        functools.partial(fused_kernel, names),
        in_specs=[smem] + [vmem] * 5,
        out_specs=[vmem] * len(outs),
        out_shape=[jax.ShapeDtypeStruct(*out[1:]) for out in outs],
        scratch_shapes=shapes,
        compiler_params=pltpu.CompilerParams(
            collective_id=2, has_side_effects=True, vmem_limit_bytes=67043328
        ),
        name="fused_block",
    )(count, hidden, cot, small0, in_rows, out_rows)


def fused_body(
    hidden_in, cotangent, lengths, norm_gain, in_weight, conv_weight, conv_bias,
    step_bias, decay_log, skip_weight, mix_gain, out_weight,
):
    small0 = jnp.zeros((16, 2 * LANES), jnp.float32)
    rows = [conv_weight, conv_bias[None], mix_gain[None], norm_gain[None], norm_gain[None, :0]]
    rows += [step_bias[None], decay_log[None], skip_weight[None]]
    at = 0
    for row in rows:
        high, wide = row.shape
        row = row.astype(jnp.float32)
        small0 = small0 + jnp.pad(row, ((at, 16 - high - at), (0, 2 * LANES - wide)))
        at += high
    full = DI + 2 * sum(side_widths())
    in_rows = jnp.pad(in_weight, ((0, 0), (0, full - in_weight.shape[1])))
    outs = run_fused(
        lengths, hidden_in, cotangent, small0, in_rows, out_weight,
        in_weight.shape, out_weight.shape,
    )
    outs = list(outs)
    for n in (2, 5, 6, 7, 8, 9):
        outs[n] = outs[n].reshape(-1)
    return tuple(outs)


def pick_body(
    hidden_in, cotangent, lengths, norm_gain, in_weight, conv_weight, conv_bias,
    step_bias, decay_log, skip_weight, mix_gain, out_weight,
):
    reps = lax.axis_size("rep")
    whole = in_weight.shape[0] % (8 * reps) == 0 and out_weight.shape[0] % (16 * reps) == 0
    whole = whole and reps > 1
    chosen = fused_body if whole and conv_bias.shape[0] <= 2 * LANES else body
    return chosen(
        hidden_in, cotangent, lengths, norm_gain, in_weight, conv_weight, conv_bias,
        step_bias, decay_log, skip_weight, mix_gain, out_weight,
    )


def solution(mesh):
    in_specs = (
        P(("fsdp", "rep"), None),
        P(("fsdp", "rep"), None),
        P(("fsdp", "rep")),
        P("fsdp"),
        P("fsdp", None),
        P(None, "fsdp"),
        P("fsdp"),
        P(),
        P(),
        P(),
        P("fsdp"),
        P("fsdp", None),
    )
    out_specs = (
        P(("fsdp", "rep"), None),
        P(("fsdp", "rep"), None),
        P("fsdp"),
        P("fsdp", None),
        P(None, "fsdp"),
        P("fsdp"),
        P(),
        P(),
        P(),
        P("fsdp"),
        P("fsdp", None),
    )
    return jax.shard_map(pick_body, mesh=mesh, in_specs=in_specs, out_specs=out_specs, check_vma=False)
```
